32 devices in a mesh: groups: 2 (over y), space: 4 (over x, core), chan: 4 (over z).
Axes of the slice: x: 2, y: 2, z: 4, core: 2. Of those that a mesh axis runs over, the one named last changes fastest.
Arguments:
- fields: bfloat16 [1024, 16, 256], P('chan', ('groups', 'space')), parts along dimension 1, may hold values from -6 to 6
- conv_weight: bfloat16 [27, 1024, 1024], P(None, 'chan', 'space'), may hold values from -0.0390625 to 0.0390625
Outputs:
- convolved: bfloat16 [1024, 16, 256], P('chan', ('groups', 'space')), parts along dimension 1
The draws below stay inside these ranges and needn't reach their ends.
There are 2 independent parts, one for each index of `groups`. The reference program is written for one: setup_inputs(seed, part) draws one part's arguments, and reference() takes and returns one part's arrays. A program takes and returns all parts, laid end to end along the dimension named above; an argument that names none is the same for every part. Nothing has to cross between parts.
All inputs are finite; a program needn't handle non-finite values.
Results may differ from the reference program's by a relative error of at most 0.001.
Values may be sent and summed in bfloat16 or wider, within the bound.
A program may use at most 128 MiB of HBM per device.

```python
import jax
import jax.numpy as jnp
from jax import lax

C = 1024
NY = 16
NZ = 16
NX = 8


def block_levels(own_key, dims, cuts, low, top_value):
    loudness, own = 1.0, jax.random.fold_in(own_key, 6)
    for dim, blocks in cuts:
        heights = jnp.exp(jax.random.uniform(jax.random.fold_in(own, dim), (blocks,), jnp.float32, low / len(cuts), top_value / len(cuts)))
        loudness = loudness * jnp.repeat(heights, dims[dim] // blocks).reshape([-1 if axis == dim else 1 for axis in range(len(dims))])
    return loudness


def noise(rng, extent, spread, reach, cuts=(), held_as=jnp.bfloat16):
    values = jax.random.normal(rng, extent, jnp.float32) * spread
    if len(cuts) > 0:
        values = block_levels(rng, extent, cuts, -0.22, 0.18) * values
    return jnp.clip(values, min=-reach, max=reach).astype(held_as)


def setup_inputs(seed: int = 0, part: int = 0) -> dict:
    arg_keys = jax.random.split(jax.random.key(seed), 3)
    own_keys = jax.random.split(jax.random.fold_in(arg_keys[2], part), 3)
    return {
        "fields": noise(own_keys[0], (C, NX, NY * NZ), 1.0, 6.0, ((0, 4), (1, 4))),
        "conv_weight": noise(arg_keys[1], (27, C, C), (27 * C) ** -0.5, 0.0390625, ((1, 4), (2, 4))),
    }


def reference(fields, conv_weight):
    depth = fields.shape[1]
    source = fields.astype(jnp.float32).reshape(C, depth, NY, NZ)
    padded = jnp.pad(source, ((0, 0), (1, 1), (1, 1), (1, 1)))
    summed = jnp.zeros((C, depth * NY * NZ), jnp.float32)
    for step_x in range(3):
        for step_y in range(3):
            for step_z in range(3):
                matrix = conv_weight[9 * step_x + 3 * step_y + step_z].astype(jnp.float32)
                window = padded[:, step_x:step_x + depth, step_y:step_y + NY, step_z:step_z + NZ].reshape(C, depth * NY * NZ)
                summed = summed + jnp.dot(matrix, window, precision=lax.Precision.HIGHEST, preferred_element_type=jnp.float32)
    return summed.reshape(C, depth, NY * NZ).astype(jnp.bfloat16)
```

```python
import functools

import jax
import jax.numpy as jnp
from jax import lax
from jax.experimental import pallas as pl
from jax.experimental.pallas import tpu as pltpu
from jax.sharding import PartitionSpec as P

NZ = 16
TAPS = 27
MESH = pl.DeviceIdType.MESH


PIECES = 4


def plan():
    return [
        ("F", 1, 0, 0), ("F", 1, 1, 0), ("P", 1, 0),
        ("F", 3, 0, 0), ("F", 2, 0, 0), ("G", 0), ("XA", 0),
        ("F", 3, 1, 0), ("F", 2, 1, 0), ("G", 1), ("XB", 0), ("XA", 1),
        ("F", 1, 2, 0), ("F", 1, 3, 0), ("P", 1, 1),
        ("F", 3, 2, 0), ("F", 2, 2, 0), ("G", 2), ("XB", 1), ("XA", 2),
        ("F", 3, 3, 0), ("F", 2, 3, 0), ("G", 3), ("XB", 2), ("XA", 3),
        ("F", 0, 0, 0), ("F", 0, 1, 0), ("XB", 3), ("P", 0, 0), ("YA", 0),
        ("F", 0, 2, 0), ("F", 0, 3, 0), ("P", 0, 1), ("YA", 1), ("YB", 0), ("YB", 1),
    ]


def first():
    return [
        ("F", 1, 0), ("R", 0), ("F", 1, 1), ("F", 3, 0), ("F", 2, 0), ("R", 1), ("F", 3, 1), ("F", 2, 1),
        ("F", 1, 2), ("R", 2), ("F", 3, 2), ("F", 2, 2), ("F", 1, 3), ("R", 3), ("F", 3, 3), ("F", 2, 3),
        ("F", 0, 0), ("F", 0, 1), ("F", 0, 2), ("F", 0, 3),
    ]


def kernel(
    S, n, x_ref, w_ref, out_ref,
    xraw, xloc, xin, xrel, xs, wv, acc, precv, orecv, xsend, xrecv,
    x_sem, w_sem, c_send, r_sem, u_send, d_send, l_send, l_recv, m_send,
    p_send, p_recv, o_send, o_recv, q_send, q_recv,
):
    chb, depth, cells = x_ref.shape
    planes = S * depth
    half = cells // 2
    piece = cells // PIECES
    stops = [0] + [(q + 1) * piece + NZ for q in range(PIECES - 1)] + [cells]
    spans = [(stops[q], stops[q + 1] - stops[q]) for q in range(PIECES)]
    s = lax.axis_index("space")
    z = lax.axis_index("chan")
    x = s // 2
    k = s % 2
    partner = 2 * x + 1 - k
    peer = 2 * (1 - x) + k
    there = 2 * (1 - x) + 1 - k
    source = s == z
    goes_up = (z >= s) & (z < n - 1)
    goes_down = (z <= s) & (z > 0)
    edge = (s == 0) | (s == n - 1)
    far_up = goes_up & (source | ~edge)
    far_down = goes_down & (source | ~edge)
    ahead = jnp.where(x == 1, 1, -1)
    origin = jnp.where(x == 1, 0, n - 1)
    feeds = z == origin
    relays = z == origin + 2 * ahead
    away = jnp.where(s == 0, z - s, s - z)

    pltpu.make_async_copy(x_ref, xraw, x_sem).start()

    barrier = pltpu.get_barrier_semaphore()

    def greet(space, chan):
        pl.semaphore_signal(
            barrier, inc=1, device_id={"space": space, "chan": chan}, device_id_type=MESH
        )

    greet(partner, z)
    greet(peer, z)

    @pl.when(z > s)
    def _():
        greet(s, z - 1)

    @pl.when(z < s)
    def _():
        greet(s, z + 1)

    @pl.when(source)
    def _():
        for so in range(1, S):
            greet(lax.rem(s + so, S), z)

    @pl.when(relays)
    def _():
        greet(s, origin)

    @pl.when(edge & (away >= 2))
    def _():
        row = jnp.where(s == 0, 2, n - 3)
        for j in range(2):
            greet(2 * (1 - x) + j, row)

    for t in range(TAPS):
        pltpu.make_async_copy(w_ref.at[t], wv.at[:, t * chb : (t + 1) * chb], w_sem.at[t]).start()

    pltpu.make_async_copy(x_ref, xraw, x_sem).wait()
    own = pltpu.einshape("cpm->pmc", xraw[...])
    xloc[...] = own

    @pl.when(source)
    def _():
        xin[s] = own

    def one(flag):
        return jnp.where(flag, 1, 0)

    pl.semaphore_wait(
        barrier,
        2 + one(~source) + one(goes_up) + one(goes_down) + one(feeds) + 2 * one(relays),
    )

    def part(ref, p, q):
        return ref.at[p, pl.ds(*spans[q])]

    def gather(p, q):
        return pltpu.make_async_remote_copy(
            src_ref=part(xloc, p, q), dst_ref=part(xin.at[s], p, q), send_sem=c_send.at[p, q],
            recv_sem=r_sem.at[s, p, q], device_id={"space": z}, device_id_type=MESH,
        )

    def feed(p, q):
        return pltpu.make_async_remote_copy(
            src_ref=part(xloc, p, q), dst_ref=part(xrel, p, q), send_sem=l_send.at[p, q],
            recv_sem=l_recv.at[p, q], device_id={"chan": z + 2 * ahead}, device_id_type=MESH,
        )

    def relay(j, p, q):
        return pltpu.make_async_remote_copy(
            src_ref=part(xrel, p, q), dst_ref=part(xin.at[s], p, q), send_sem=m_send.at[j, p, q],
            recv_sem=r_sem.at[s, p, q], device_id={"space": origin, "chan": z + j * ahead},
            device_id_type=MESH,
        )

    def lane(b, p, q, sem, to):
        view = part(xin.at[b], p, q)
        return pltpu.make_async_remote_copy(
            src_ref=view, dst_ref=view, send_sem=sem.at[b, p, q], recv_sem=r_sem.at[b, p, q],
            device_id={"chan": to}, device_id_type=MESH,
        )

    def block(o):
        return jnp.where(x == 0, o, S - 1 - o)

    for q in range(PIECES):
        for p in range(depth):
            @pl.when(feeds)
            def _():
                feed(p, q).start()

            @pl.when(~source)
            def _():
                gather(p, q).start()

    def fetch(o, q):
        b = block(o)
        for p in range(depth):
            @pl.when(b != jnp.where(source, s, S))
            def _():
                lane(b, p, q, u_send, lax.rem(z + 1, n)).wait_recv()

            @pl.when(far_up if o >= 2 else goes_up)
            def _():
                lane(b, p, q, u_send, z + 1).start()

            @pl.when(far_down if o >= 2 else goes_down)
            def _():
                lane(b, p, q, d_send, z - 1).start()

    def pass_piece(q):
        for p in range(depth):
            feed(p, q).wait_recv()
            for j in (1, 0):
                relay(j, p, q).start()

    def shifted(b, start, size):
        rows = lax.broadcasted_iota(jnp.int32, (size, chb), 0) % NZ
        to = slice(NZ + start, NZ + start + size)
        for p in range(depth):
            v = xin[b, p, start : start + size, :]
            wide = v.astype(jnp.float32)
            before = jnp.where(rows == 0, 0.0, pltpu.roll(wide, 1, 0))
            after = jnp.where(rows == NZ - 1, 0.0, pltpu.roll(wide, size - 1, 0))
            at = b * depth + p
            xs[at, 0, to, :] = before.astype(xs.dtype)
            xs[at, 1, to, :] = v
            xs[at, 2, to, :] = after.astype(xs.dtype)

    def multiply(base, count, start, size):
        window = jnp.concatenate(
            [
                jnp.concatenate(
                    [xs[base + p, c, NZ * y + start : NZ * y + start + size, :] for p in range(count)],
                    axis=0,
                )
                for y in range(3)
                for c in range(3)
            ],
            axis=1,
        )
        for a in range(3):
            terms = lax.dot_general(
                window, wv[:, a * 9 * chb : (a + 1) * 9 * chb], (((1,), (1,)), ((), ())),
                preferred_element_type=jnp.float32,
            )
            acc[pl.ds(base + 2 - a, count), start : start + size, :] += terms.reshape(
                count, size, chb
            )

    def near(o, h):
        b = block(o)
        start = 0 if h == 0 else stops[PIECES // 2]
        stop = stops[PIECES // 2] if h == 0 else cells
        shifted(b, start, stop - start)
        multiply(b * depth, depth, h * half, half)

    def distant(q):
        for o in (3, 2):
            shifted(block(o), *spans[q])
        multiply(2 * (1 - x) * depth, 2 * depth, q * piece, piece)

    def sums(core, start, size):
        return acc.at[pl.ds(core * depth + 1, depth), start : start + size]

    def far_piece(q):
        return pltpu.make_async_remote_copy(
            src_ref=sums(there, q * piece, piece), dst_ref=precv.at[q],
            send_sem=p_send.at[q], recv_sem=p_recv.at[q],
            device_id={"space": partner}, device_id_type=MESH,
        )

    def own_half(h):
        return pltpu.make_async_remote_copy(
            src_ref=sums(partner, h * half, half), dst_ref=orecv.at[h],
            send_sem=o_send.at[h], recv_sem=o_recv.at[h],
            device_id={"space": partner}, device_id_type=MESH,
        )

    def across(q):
        return pltpu.make_async_remote_copy(
            src_ref=xsend.at[q], dst_ref=xrecv.at[q], send_sem=q_send.at[q], recv_sem=q_recv.at[q],
            device_id={"space": peer}, device_id_type=MESH,
        )

    def pass_on(q):
        far_piece(q).wait_recv()
        xsend[q] = sums(peer, q * piece, piece)[...] + precv[q]
        across(q).start()

    def finish(h):
        own_half(h).wait_recv()
        total = sums(s, h * half, half)[...] + orecv[h]
        for j in range(PIECES // 2):
            across(h * PIECES // 2 + j).wait_recv()
        far = jnp.concatenate([xrecv[h * PIECES // 2 + j] for j in range(PIECES // 2)], axis=1)
        total = total + far
        wide = jnp.concatenate([total[p].T for p in range(depth)], axis=1)
        out_ref[:, :, h * half : (h + 1) * half] = wide.reshape(chb, depth, half).astype(
            out_ref.dtype
        )

    @pl.when(source)
    def _():
        for op in first():
            if op[0] == "F":
                fetch(*op[1:])
            else:
                @pl.when(relays)
                def _():
                    pass_piece(op[1])

    zero_row = jnp.zeros((NZ, chb), xs.dtype)
    for at in range(planes):
        for c in range(3):
            xs[at, c, :NZ, :] = zero_row
            xs[at, c, NZ + cells :, :] = zero_row
    for at in range(planes + 2):
        acc[at] = jnp.zeros(acc.shape[1:], acc.dtype)

    ready = False
    for op in plan():
        if op[0] == "F":
            @pl.when(~source)
            def _():
                fetch(op[1], op[2])
                if op[1] == 3:
                    @pl.when(relays)
                    def _():
                        pass_piece(op[2])
        if op[0] in ("P", "G") and not ready:
            ready = True
            for t in range(TAPS):
                pltpu.make_async_copy(
                    w_ref.at[t], wv.at[:, t * chb : (t + 1) * chb], w_sem.at[t]
                ).wait()
        if op[0] == "P":
            near(*op[1:])
        if op[0] == "G":
            distant(op[1])
        if op[0] == "XA":
            far_piece(op[1]).start()
        if op[0] == "XB":
            pass_on(op[1])
        if op[0] == "YA":
            own_half(op[1]).start()
        if op[0] == "YB":
            finish(op[1])

    for q in range(PIECES):
        for p in range(depth):
            @pl.when(feeds)
            def _():
                feed(p, q).wait_send()

            @pl.when(~source)
            def _():
                gather(p, q).wait_send()

            @pl.when(relays)
            def _():
                for j in range(2):
                    relay(j, p, q).wait_send()

            for o in range(S):
                @pl.when(far_up if o >= 2 else goes_up)
                def _():
                    lane(block(o), p, q, u_send, lax.rem(z + 1, n)).wait_send()

                @pl.when(far_down if o >= 2 else goes_down)
                def _():
                    lane(block(o), p, q, d_send, lax.rem(z + n - 1, n)).wait_send()

        far_piece(q).wait_send()
        across(q).wait_send()
    for h in range(2):
        own_half(h).wait_send()


def local(S, n, fields, conv_weight):
    chb, depth, cells = fields.shape
    owned, I = conv_weight.shape[1:]
    if not (S == n == 4 and owned == I == chb):
        return general(S, n, fields, conv_weight)
    planes = S * depth
    bf16, f32 = jnp.bfloat16, jnp.float32
    dma = pltpu.SemaphoreType.DMA
    piece = cells // PIECES
    return pl.pallas_call(
        functools.partial(kernel, S, n),
        out_shape=jax.ShapeDtypeStruct((owned, depth, cells), bf16),
        in_specs=[pl.BlockSpec(memory_space=pl.ANY), pl.BlockSpec(memory_space=pl.ANY)],
        out_specs=pl.BlockSpec(memory_space=pltpu.VMEM),
        scratch_shapes=[
            pltpu.VMEM((chb, depth, cells), bf16),
            pltpu.VMEM((depth, cells, chb), bf16),
            pltpu.VMEM((S, depth, cells, chb), bf16),
            pltpu.VMEM((depth, cells, chb), bf16),
            pltpu.VMEM((planes, 3, cells + 2 * NZ, chb), bf16),
            pltpu.VMEM((owned, TAPS * chb), bf16),
            pltpu.VMEM((planes + 2, cells, owned), f32),
            pltpu.VMEM((PIECES, depth, piece, owned), f32),
            pltpu.VMEM((2, depth, cells // 2, owned), f32),
            pltpu.VMEM((PIECES, depth, piece, owned), f32),
            pltpu.VMEM((PIECES, depth, piece, owned), f32),
            dma(()),
            dma((TAPS,)),
            dma((depth, PIECES)),
            dma((S, depth, PIECES)),
            dma((S, depth, PIECES)),
            dma((S, depth, PIECES)),
            dma((depth, PIECES)),
            dma((depth, PIECES)),
            dma((2, depth, PIECES)),
            dma((PIECES,)),
            dma((PIECES,)),
            dma((2,)),
            dma((2,)),
            dma((PIECES,)),
            dma((PIECES,)),
        ],
        compiler_params=pltpu.CompilerParams(
            collective_id=0, has_side_effects=True, vmem_limit_bytes=62 * 1024 * 1024
        ),
    )(fields, conv_weight)


def general_kernel(
    S, n, r, x_ref, w_ref, out_ref,
    xz, xr, xs, wv, psend, precv, xsend, xrecv, own,
    w_sem, up_sem, down_sem, z_sem, a_send, a_recv, p_send, p_recv, q_send, q_recv,
):
    depth, cells, chb = x_ref.shape
    I = r * chb
    nx = S // 2
    planes = S * depth
    s = lax.axis_index("space")
    z = lax.axis_index("chan")
    x = s // 2
    k = s % 2
    partner = x * 2 + (1 - k)

    for t in range(TAPS):
        pltpu.make_async_copy(w_ref.at[t], wv.at[:, t * I : (t + 1) * I], w_sem.at[t]).start()

    barrier = pltpu.get_barrier_semaphore()

    for so in range(S):
        for step, there in ((-1, z > 0), (1, z < n - 1)):
            @pl.when(there)
            def _():
                pl.semaphore_signal(
                    barrier, inc=1, device_id={"space": lax.rem(s + so, S), "chan": z + step},
                    device_id_type=MESH,
                )

    for so in range(1, S):
        pl.semaphore_signal(
            barrier, inc=1, device_id={"space": lax.rem(s + so, S)}, device_id_type=MESH
        )
    here = jnp.where(z > 0, S, 0) + jnp.where(z < n - 1, S, 0) + (S - 1)
    pl.semaphore_wait(barrier, here)

    split = cells // 2 + NZ
    spans = ((0, split), (split, cells - split))
    rows_out = cells // 2

    def part(ref, u):
        return ref.at[u % depth, pl.ds(*spans[u // depth])]

    def hop(src, b, p, sem, to):
        return pltpu.make_async_remote_copy(
            src_ref=src, dst_ref=part(xz.at[b], p), send_sem=sem, recv_sem=z_sem.at[b, p],
            device_id={"chan": to}, device_id_type=MESH,
        )

    def across(src, b, p):
        return pltpu.make_async_remote_copy(
            src_ref=src, dst_ref=part(xr.at[s, b % r], p), send_sem=a_send.at[b, p],
            recv_sem=a_recv.at[s, b % r, p],
            device_id={"space": b // r}, device_id_type=MESH,
        )

    def source(h, b, p):
        return part(x_ref, p) if h == 0 else part(xz.at[b], p)

    def up(h, p):
        return hop(source(h, z - h, p), z - h, p, up_sem.at[h, p], z + 1)

    def down(h, p):
        return hop(source(h, z + h, p), z + h, p, down_sem.at[h, p], z - 1)

    def slanted(h, b, p, sem, to):
        return pltpu.make_async_remote_copy(
            src_ref=source(h, b, p), dst_ref=part(xr.at[s, b % r], p), send_sem=sem,
            recv_sem=a_recv.at[s, b % r, p],
            device_id={"space": b // r, "chan": to}, device_id_type=MESH,
        )

    def direct(h, b, to, end):
        return (to == end) & (b // r != s)

    def forward(h, p):
        for b, sign, end, send in ((z - h, 1, n - 1, up), (z + h, -1, 0, down)):
            valid = (b >= 0) & (b < n)
            relay = valid
            if h > 0:
                relay = valid & (z != end)

                @pl.when(relay)
                def _():
                    hop(part(xz.at[b], p), b, p, up_sem.at[0, p], z).wait_recv()

            if h < n - 1:
                straight = direct(h, b, z + sign, end)

                @pl.when(valid & (z != end) & ~straight)
                def _():
                    send(h, p).start()

                @pl.when(valid & (z != end) & straight)
                def _():
                    sem = (up_sem if sign == 1 else down_sem).at[h, p]
                    slanted(h, b, p, sem, z + sign).start()

            if h > 0 or sign == 1:
                @pl.when(relay & (b // r != s))
                def _():
                    across(source(h, b, p), b, p).start()

    for p in range(2 * depth):
        forward(0, p)

    zero_row = jnp.zeros((NZ, I), xs.dtype)
    zero_plane = jnp.zeros(xs.shape[2:], xs.dtype)
    for c in range(3):
        xs[0, c] = zero_plane
        xs[planes + 1, c] = zero_plane

        @pl.loop(1, planes + 1)
        def _(q):
            xs[q, c, :NZ, :] = zero_row
            xs[q, c, NZ + cells :, :] = zero_row

    def prepare(ref, u, q, j):
        v = part(ref, u)[...]
        start, size = spans[u // depth]
        rows = lax.broadcasted_iota(jnp.int32, (size, chb), 0) % NZ
        wide = v.astype(jnp.float32)
        before = jnp.where(rows == 0, 0.0, pltpu.roll(wide, 1, 0))
        after = jnp.where(rows == NZ - 1, 0.0, pltpu.roll(wide, size - 1, 0))
        lanes = slice(j * chb, (j + 1) * chb)
        to = slice(NZ + start, NZ + start + size)
        xs[q + 1, 0, to, lanes] = before.astype(xs.dtype)
        xs[q + 1, 1, to, lanes] = v
        xs[q + 1, 2, to, lanes] = after.astype(xs.dtype)

    for half in range(2):
        for h in range(1, n - 1):
            for p in range(depth):
                forward(h, half * depth + p)

    def fetch_half(half):
        for p in range(depth):
            u = half * depth + p
            for j in range(r):
                @pl.when(z == s * r + j)
                def _():
                    prepare(x_ref, u, s * depth + p, j)

                b = s * r + j

                @pl.when(((z == 0) & (b > 0)) | ((z == n - 1) & (b < n - 1)))
                def _():
                    hop(part(xz.at[b], u), b, u, up_sem.at[0, u], z).wait_recv()

                @pl.when(z != s * r + j)
                def _():
                    prepare(xz.at[s * r + j], u, s * depth + p, j)

            @pl.loop(1, S)
            def _(so):
                src = lax.rem(s + so, S)
                for j in range(r):
                    view = part(xr.at[src, j], u)
                    pltpu.make_async_remote_copy(
                        src_ref=view, dst_ref=view,
                        send_sem=a_send.at[0, u], recv_sem=a_recv.at[src, j, u],
                        device_id={"space": src}, device_id_type=MESH,
                    ).wait_recv()
                    prepare(xr.at[src, j], u, src * depth + p, j)

    for t in range(TAPS):
        pltpu.make_async_copy(w_ref.at[t], wv.at[:, t * I : (t + 1) * I], w_sem.at[t]).wait()

    def partial(dest, half):
        window = jnp.concatenate(
            [
                jnp.concatenate(
                    [
                        xs[
                            dest * depth + p + a, c,
                            NZ * b + half * rows_out : NZ * b + (half + 1) * rows_out, :,
                        ]
                        for p in range(depth)
                    ],
                    axis=0,
                )
                for a in range(3)
                for b in range(3)
                for c in range(3)
            ],
            axis=1,
        )
        return lax.dot_general(
            window, wv[...], (((1,), (1,)), ((), ())), preferred_element_type=jnp.float32
        )

    def target(hops, mine):
        far = lax.rem(x + hops, nx)
        return far * 2 + jnp.where(mine == 1, k, 1 - k)

    def half_of(ref, m, half):
        return ref.at[m, half]

    def to_partner(m, half):
        return pltpu.make_async_remote_copy(
            src_ref=half_of(psend, m, half), dst_ref=half_of(precv, m, half),
            send_sem=p_send.at[m, half], recv_sem=p_recv.at[m, half],
            device_id={"space": partner}, device_id_type=MESH,
        )

    def to_chip(m, half, there):
        return pltpu.make_async_remote_copy(
            src_ref=half_of(xsend, m, half), dst_ref=half_of(xrecv, m, half),
            send_sem=q_send.at[m, half], recv_sem=q_recv.at[m, half],
            device_id={"space": there}, device_id_type=MESH,
        )

    def reduce_half(half, first, stop):
        @pl.loop(2 * first, 2 * stop)
        def _(i):
            m = i // 2
            mine = i % 2
            total = partial(target(m + 1, mine), half)

            @pl.when(mine == 0)
            def _():
                psend[m, half] = total
                to_partner(m, half).start()

            @pl.when(mine == 1)
            def _():
                to_partner(m, half).wait_recv()
                if first < nx - 1:
                    xsend[m, half] = total + precv[m, half]
                    to_chip(m, half, target(m + 1, 1)).start()
                else:
                    own[half] = total + precv[m, half]

    fetch_half(0)
    reduce_half(0, 0, nx - 1)
    fetch_half(1)
    reduce_half(1, 0, nx - 1)
    for half in range(2):
        reduce_half(half, nx - 1, nx)

    for half in range(2):
        total = own[half]
        for m in range(nx - 1):
            to_chip(m, half, partner).wait_recv()
            total = total + xrecv[m, half]
        for p in range(depth):
            out_ref[p, half * rows_out : (half + 1) * rows_out, :] = total[
                p * rows_out : (p + 1) * rows_out
            ].astype(out_ref.dtype)

    for h in range(n):
        for p in range(2 * depth):
            if h < n - 1:
                @pl.when((z - h >= 0) & (z < n - 1))
                def _():
                    up(h, p).wait_send()

                @pl.when((z + h < n) & (z > 0))
                def _():
                    down(h, p).wait_send()

            for b, sign, end in ((z - h, 1, n - 1), (z + h, -1, 0)):
                relay = (b >= 0) & (b < n) & (b // r != s)
                if h > 0:
                    relay = relay & ~direct(h - 1, b, z, end)

                if h > 0 or sign == 1:
                    @pl.when(relay)
                    def _():
                        across(source(h, b, p), b, p).wait_send()

    for m in range(nx):
        for half in range(2):
            to_partner(m, half).wait_send()
            if m < nx - 1:
                to_chip(m, half, partner).wait_send()


def general(S, n, fields, conv_weight):
    chb, depth, cells = fields.shape
    owned, I = conv_weight.shape[1:]
    r = I // chb
    nx = S // 2
    planes = S * depth
    bf16, f32 = jnp.bfloat16, jnp.float32
    dma = pltpu.SemaphoreType.DMA
    x = jnp.transpose(fields, (1, 2, 0))
    result = pl.pallas_call(
        functools.partial(general_kernel, S, n, r),
        out_shape=jax.ShapeDtypeStruct((depth, cells, owned), bf16),
        in_specs=[
            pl.BlockSpec(memory_space=pltpu.VMEM),
            pl.BlockSpec(memory_space=pl.ANY),
        ],
        out_specs=pl.BlockSpec(memory_space=pltpu.VMEM),
        scratch_shapes=[
            pltpu.VMEM((n, depth, cells, chb), bf16),
            pltpu.VMEM((S, r, depth, cells, chb), bf16),
            pltpu.VMEM((planes + 2, 3, cells + 2 * NZ, I), bf16),
            pltpu.VMEM((owned, TAPS * I), bf16),
            pltpu.VMEM((nx, 2, depth * cells // 2, owned), f32),
            pltpu.VMEM((nx, 2, depth * cells // 2, owned), f32),
            pltpu.VMEM((nx - 1, 2, depth * cells // 2, owned), f32),
            pltpu.VMEM((nx - 1, 2, depth * cells // 2, owned), f32),
            pltpu.VMEM((2, depth * cells // 2, owned), f32),
            dma((TAPS,)),
            dma((n, 2 * depth)),
            dma((n, 2 * depth)),
            dma((n, 2 * depth)),
            dma((n, 2 * depth)),
            dma((S, r, 2 * depth)),
            dma((nx, 2)),
            dma((nx, 2)),
            dma((nx, 2)),
            dma((nx, 2)),
        ],
        compiler_params=pltpu.CompilerParams(
            collective_id=0, has_side_effects=True, vmem_limit_bytes=62 * 1024 * 1024
        ),
    )(x, conv_weight)
    return jnp.transpose(result, (2, 0, 1))


def solution(mesh):
    return jax.shard_map(
        functools.partial(local, mesh.shape["space"], mesh.shape["chan"]),
        mesh=mesh,
        in_specs=(P("chan", ("groups", "space"), None), P(None, "chan", "space")),
        out_specs=P("chan", ("groups", "space"), None),
        check_vma=False,
    )
```

```python
import functools

import jax
import jax.numpy as jnp
from jax import lax
from jax.experimental import pallas as pl
from jax.experimental.pallas import tpu as pltpu
from jax.sharding import PartitionSpec as P

NZ = 16
TAPS = 27
MESH = pl.DeviceIdType.MESH


PIECES = 4


def plan():
    return [
        ("F", 1, 0, 0), ("F", 1, 1, 0), ("P", 1, 0),
        ("F", 3, 0, 0), ("F", 2, 0, 0), ("G", 0), ("XA", 0),
        ("F", 3, 1, 0), ("F", 2, 1, 0), ("G", 1), ("XB", 0), ("XA", 1),
        ("F", 1, 2, 0), ("F", 1, 3, 0), ("P", 1, 1),
        ("F", 3, 2, 0), ("F", 2, 2, 0), ("G", 2), ("XB", 1), ("XA", 2),
        ("F", 3, 3, 0), ("F", 2, 3, 0), ("G", 3), ("XB", 2), ("XA", 3),
        ("F", 0, 0, 0), ("F", 0, 1, 0), ("XB", 3), ("P", 0, 0), ("YA", 0),
        ("F", 0, 2, 0), ("F", 0, 3, 0), ("P", 0, 1), ("YA", 1), ("YB", 0), ("YB", 1),
    ]


def first():
    return [
        ("F", 1, 0), ("R", 0), ("F", 1, 1), ("F", 3, 0), ("F", 2, 0), ("R", 1), ("F", 3, 1), ("F", 2, 1),
        ("F", 1, 2), ("R", 2), ("F", 3, 2), ("F", 2, 2), ("F", 1, 3), ("R", 3), ("F", 3, 3), ("F", 2, 3),
        ("F", 0, 0), ("F", 0, 1), ("F", 0, 2), ("F", 0, 3),
    ]


def kernel(
    S, n, x_ref, w_ref, out_ref,
    xraw, xloc, xin, xrel, xs, wv, acc, precv, orecv, xsend, xrecv,
    x_sem, w_sem, c_send, r_sem, u_send, d_send, l_send, l_recv, m_send,
    p_send, p_recv, o_send, o_recv, q_send, q_recv,
):
    chb, depth, cells = x_ref.shape
    planes = S * depth
    half = cells // 2
    piece = cells // PIECES
    stops = [0] + [(q + 1) * piece + NZ for q in range(PIECES - 1)] + [cells]
    spans = [(stops[q], stops[q + 1] - stops[q]) for q in range(PIECES)]
    s = lax.axis_index("space")
    z = lax.axis_index("chan")
    x = s // 2
    k = s % 2
    partner = 2 * x + 1 - k
    peer = 2 * (1 - x) + k
    there = 2 * (1 - x) + 1 - k
    source = s == z
    goes_up = (z >= s) & (z < n - 1)
    goes_down = (z <= s) & (z > 0)
    edge = (s == 0) | (s == n - 1)
    far_up = goes_up & (source | ~edge)
    far_down = goes_down & (source | ~edge)
    ahead = jnp.where(x == 1, 1, -1)
    origin = jnp.where(x == 1, 0, n - 1)
    feeds = z == origin
    relays = z == origin + 2 * ahead
    away = jnp.where(s == 0, z - s, s - z)

    pltpu.make_async_copy(x_ref, xraw, x_sem).start()

    barrier = pltpu.get_barrier_semaphore()

    def greet(space, chan):
        pl.semaphore_signal(
            barrier, inc=1, device_id={"space": space, "chan": chan}, device_id_type=MESH
        )

    greet(partner, z)
    greet(peer, z)

    @pl.when(z > s)
    def _():
        greet(s, z - 1)

    @pl.when(z < s)
    def _():
        greet(s, z + 1)

    @pl.when(source)
    def _():
        for so in range(1, S):
            greet(lax.rem(s + so, S), z)

    @pl.when(relays)
    def _():
        greet(s, origin)

    @pl.when(edge & (away >= 2))
    def _():
        row = jnp.where(s == 0, 2, n - 3)
        for j in range(2):
            greet(2 * (1 - x) + j, row)

    for t in range(TAPS):
        pltpu.make_async_copy(w_ref.at[t], wv.at[:, t * chb : (t + 1) * chb], w_sem.at[t]).start()

    pltpu.make_async_copy(x_ref, xraw, x_sem).wait()
    own = pltpu.einshape("cpm->pmc", xraw[...])
    xloc[...] = own

    @pl.when(source)
    def _():
        xin[s] = own

    def one(flag):
        return jnp.where(flag, 1, 0)

    pl.semaphore_wait(
        barrier,
        2 + one(~source) + one(goes_up) + one(goes_down) + one(feeds) + 2 * one(relays),
    )

    def part(ref, p, q):
        return ref.at[p, pl.ds(*spans[q])]

    def gather(p, q):
        return pltpu.make_async_remote_copy(
            src_ref=part(xloc, p, q), dst_ref=part(xin.at[s], p, q), send_sem=c_send.at[p, q],
            recv_sem=r_sem.at[s, p, q], device_id={"space": z}, device_id_type=MESH,
        )

    def feed(p, q):
        return pltpu.make_async_remote_copy(
            src_ref=part(xloc, p, q), dst_ref=part(xrel, p, q), send_sem=l_send.at[p, q],
            recv_sem=l_recv.at[p, q], device_id={"chan": z + 2 * ahead}, device_id_type=MESH,
        )

    def relay(j, p, q):
        return pltpu.make_async_remote_copy(
            src_ref=part(xrel, p, q), dst_ref=part(xin.at[s], p, q), send_sem=m_send.at[j, p, q],
            recv_sem=r_sem.at[s, p, q], device_id={"space": origin, "chan": z + j * ahead},
            device_id_type=MESH,
        )

    def lane(b, p, q, sem, to):
        view = part(xin.at[b], p, q)
        return pltpu.make_async_remote_copy(
            src_ref=view, dst_ref=view, send_sem=sem.at[b, p, q], recv_sem=r_sem.at[b, p, q],
            device_id={"chan": to}, device_id_type=MESH,
        )

    def block(o):
        return jnp.where(x == 0, o, S - 1 - o)

    for q in range(PIECES):
        for p in range(depth):
            @pl.when(feeds)
            def _():
                feed(p, q).start()

            @pl.when(~source)
            def _():
                gather(p, q).start()

    def fetch(o, q):
        b = block(o)
        for p in range(depth):
            @pl.when(b != jnp.where(source, s, S))
            def _():
                lane(b, p, q, u_send, lax.rem(z + 1, n)).wait_recv()

            @pl.when(far_up if o >= 2 else goes_up)
            def _():
                lane(b, p, q, u_send, z + 1).start()

            @pl.when(far_down if o >= 2 else goes_down)
            def _():
                lane(b, p, q, d_send, z - 1).start()

    def pass_piece(q):
        for p in range(depth):
            feed(p, q).wait_recv()
            for j in (1, 0):
                relay(j, p, q).start()

    def shifted(b, start, size):
        rows = lax.broadcasted_iota(jnp.int32, (size, chb), 0) % NZ
        to = slice(NZ + start, NZ + start + size)
        for p in range(depth):
            v = xin[b, p, start : start + size, :]
            wide = v.astype(jnp.float32)
            before = jnp.where(rows == 0, 0.0, pltpu.roll(wide, 1, 0))
            after = jnp.where(rows == NZ - 1, 0.0, pltpu.roll(wide, size - 1, 0))
            at = b * depth + p
            xs[at, 0, to, :] = before.astype(xs.dtype)
            xs[at, 1, to, :] = v
            xs[at, 2, to, :] = after.astype(xs.dtype)

    def multiply(base, count, start, size):
        window = jnp.concatenate(
            [
                jnp.concatenate(
                    [xs[base + p, c, NZ * y + start : NZ * y + start + size, :] for p in range(count)],
                    axis=0,
                )
                for y in range(3)
                for c in range(3)
            ],
            axis=1,
        )
        for a in range(3):
            terms = lax.dot_general(
                window, wv[:, a * 9 * chb : (a + 1) * 9 * chb], (((1,), (1,)), ((), ())),
                preferred_element_type=jnp.float32,
            )
            acc[pl.ds(base + 2 - a, count), start : start + size, :] += terms.reshape(
                count, size, chb
            )

    def near(o, h):
        b = block(o)
        start = 0 if h == 0 else stops[PIECES // 2]
        stop = stops[PIECES // 2] if h == 0 else cells
        shifted(b, start, stop - start)
        multiply(b * depth, depth, h * half, half)

    def distant(q):
        for o in (3, 2):
            shifted(block(o), *spans[q])
        multiply(2 * (1 - x) * depth, 2 * depth, q * piece, piece)

    def sums(core, start, size):
        return acc.at[pl.ds(core * depth + 1, depth), start : start + size]

    def far_piece(q):
        return pltpu.make_async_remote_copy(
            src_ref=sums(there, q * piece, piece), dst_ref=precv.at[q],
            send_sem=p_send.at[q], recv_sem=p_recv.at[q],
            device_id={"space": partner}, device_id_type=MESH,
        )

    def own_half(h):
        return pltpu.make_async_remote_copy(
            src_ref=sums(partner, h * half, half), dst_ref=orecv.at[h],
            send_sem=o_send.at[h], recv_sem=o_recv.at[h],
            device_id={"space": partner}, device_id_type=MESH,
        )

    def across(q):
        return pltpu.make_async_remote_copy(
            src_ref=xsend.at[q], dst_ref=xrecv.at[q], send_sem=q_send.at[q], recv_sem=q_recv.at[q],
            device_id={"space": peer}, device_id_type=MESH,
        )

    def pass_on(q):
        far_piece(q).wait_recv()
        xsend[q] = sums(peer, q * piece, piece)[...] + precv[q]
        across(q).start()

    def finish(h):
        own_half(h).wait_recv()
        total = sums(s, h * half, half)[...] + orecv[h]
        for j in range(PIECES // 2):
            across(h * PIECES // 2 + j).wait_recv()
        far = jnp.concatenate([xrecv[h * PIECES // 2 + j] for j in range(PIECES // 2)], axis=1)
        total = total + far
        wide = jnp.concatenate([total[p].T for p in range(depth)], axis=1)
        out_ref[:, :, h * half : (h + 1) * half] = wide.reshape(chb, depth, half).astype(
            out_ref.dtype
        )

    @pl.when(source)
    def _():
        for op in first():
            if op[0] == "F":
                fetch(*op[1:])
            else:
                @pl.when(relays)
                def _():
                    pass_piece(op[1])

    zero_row = jnp.zeros((NZ, chb), xs.dtype)
    for at in range(planes):
        for c in range(3):
            xs[at, c, :NZ, :] = zero_row
            xs[at, c, NZ + cells :, :] = zero_row
    for at in range(planes + 2):
        acc[at] = jnp.zeros(acc.shape[1:], acc.dtype)

    ready = False
    for op in plan():
        if op[0] == "F":
            @pl.when(~source)
            def _():
                fetch(op[1], op[2])
                if op[1] == 3:
                    @pl.when(relays)
                    def _():
                        pass_piece(op[2])
        if op[0] in ("P", "G") and not ready:
            ready = True
            for t in range(TAPS):
                pltpu.make_async_copy(
                    w_ref.at[t], wv.at[:, t * chb : (t + 1) * chb], w_sem.at[t]
                ).wait()
        if op[0] == "P":
            near(*op[1:])
        if op[0] == "G":
            distant(op[1])
        if op[0] == "XA":
            far_piece(op[1]).start()
        if op[0] == "XB":
            pass_on(op[1])
        if op[0] == "YA":
            own_half(op[1]).start()
        if op[0] == "YB":
            finish(op[1])

    for q in range(PIECES):
        for p in range(depth):
            @pl.when(feeds)
            def _():
                feed(p, q).wait_send()

            @pl.when(~source)
            def _():
                gather(p, q).wait_send()

            @pl.when(relays)
            def _():
                for j in range(2):
                    relay(j, p, q).wait_send()

            for o in range(S):
                @pl.when(far_up if o >= 2 else goes_up)
                def _():
                    lane(block(o), p, q, u_send, lax.rem(z + 1, n)).wait_send()

                @pl.when(far_down if o >= 2 else goes_down)
                def _():
                    lane(block(o), p, q, d_send, lax.rem(z + n - 1, n)).wait_send()

        far_piece(q).wait_send()
        across(q).wait_send()
    for h in range(2):
        own_half(h).wait_send()


def local(S, n, fields, conv_weight):
    chb, depth, cells = fields.shape
    owned, I = conv_weight.shape[1:]
    if not (S == n == 4 and owned == I == chb):
        return general(S, n, fields, conv_weight)
    planes = S * depth
    bf16, f32 = jnp.bfloat16, jnp.float32
    dma = pltpu.SemaphoreType.DMA
    piece = cells // PIECES
    return pl.pallas_call(
        functools.partial(kernel, S, n),
        out_shape=pltpu.VMEM((owned, depth, cells), bf16),
        in_specs=[pl.BlockSpec(memory_space=pl.ANY), pl.BlockSpec(memory_space=pl.ANY)],
        out_specs=pl.BlockSpec(memory_space=pltpu.VMEM),
        scratch_shapes=[
            pltpu.VMEM((chb, depth, cells), bf16),
            pltpu.VMEM((depth, cells, chb), bf16),
            pltpu.VMEM((S, depth, cells, chb), bf16),
            pltpu.VMEM((depth, cells, chb), bf16),
            pltpu.VMEM((planes, 3, cells + 2 * NZ, chb), bf16),
            pltpu.VMEM((owned, TAPS * chb), bf16),
            pltpu.VMEM((planes + 2, cells, owned), f32),
            pltpu.VMEM((PIECES, depth, piece, owned), f32),
            pltpu.VMEM((2, depth, cells // 2, owned), f32),
            pltpu.VMEM((PIECES, depth, piece, owned), f32),
            pltpu.VMEM((PIECES, depth, piece, owned), f32),
            dma(()),
            dma((TAPS,)),
            dma((depth, PIECES)),
            dma((S, depth, PIECES)),
            dma((S, depth, PIECES)),
            dma((S, depth, PIECES)),
            dma((depth, PIECES)),
            dma((depth, PIECES)),
            dma((2, depth, PIECES)),
            dma((PIECES,)),
            dma((PIECES,)),
            dma((2,)),
            dma((2,)),
            dma((PIECES,)),
            dma((PIECES,)),
        ],
        compiler_params=pltpu.CompilerParams(
            collective_id=0, has_side_effects=True, vmem_limit_bytes=62 * 1024 * 1024
        ),
    )(fields, conv_weight)


def general_kernel(
    S, n, r, x_ref, w_ref, out_ref,
    xz, xr, xs, wv, psend, precv, xsend, xrecv, own,
    w_sem, up_sem, down_sem, z_sem, a_send, a_recv, p_send, p_recv, q_send, q_recv,
):
    depth, cells, chb = x_ref.shape
    I = r * chb
    nx = S // 2
    planes = S * depth
    s = lax.axis_index("space")
    z = lax.axis_index("chan")
    x = s // 2
    k = s % 2
    partner = x * 2 + (1 - k)

    for t in range(TAPS):
        pltpu.make_async_copy(w_ref.at[t], wv.at[:, t * I : (t + 1) * I], w_sem.at[t]).start()

    barrier = pltpu.get_barrier_semaphore()

    for so in range(S):
        for step, there in ((-1, z > 0), (1, z < n - 1)):
            @pl.when(there)
            def _():
                pl.semaphore_signal(
                    barrier, inc=1, device_id={"space": lax.rem(s + so, S), "chan": z + step},
                    device_id_type=MESH,
                )

    for so in range(1, S):
        pl.semaphore_signal(
            barrier, inc=1, device_id={"space": lax.rem(s + so, S)}, device_id_type=MESH
        )
    here = jnp.where(z > 0, S, 0) + jnp.where(z < n - 1, S, 0) + (S - 1)
    pl.semaphore_wait(barrier, here)

    split = cells // 2 + NZ
    spans = ((0, split), (split, cells - split))
    rows_out = cells // 2

    def part(ref, u):
        return ref.at[u % depth, pl.ds(*spans[u // depth])]

    def hop(src, b, p, sem, to):
        return pltpu.make_async_remote_copy(
            src_ref=src, dst_ref=part(xz.at[b], p), send_sem=sem, recv_sem=z_sem.at[b, p],
            device_id={"chan": to}, device_id_type=MESH,
        )

    def across(src, b, p):
        return pltpu.make_async_remote_copy(
            src_ref=src, dst_ref=part(xr.at[s, b % r], p), send_sem=a_send.at[b, p],
            recv_sem=a_recv.at[s, b % r, p],
            device_id={"space": b // r}, device_id_type=MESH,
        )

    def source(h, b, p):
        return part(x_ref, p) if h == 0 else part(xz.at[b], p)

    def up(h, p):
        return hop(source(h, z - h, p), z - h, p, up_sem.at[h, p], z + 1)

    def down(h, p):
        return hop(source(h, z + h, p), z + h, p, down_sem.at[h, p], z - 1)

    def slanted(h, b, p, sem, to):
        return pltpu.make_async_remote_copy(
            src_ref=source(h, b, p), dst_ref=part(xr.at[s, b % r], p), send_sem=sem,
            recv_sem=a_recv.at[s, b % r, p],
            device_id={"space": b // r, "chan": to}, device_id_type=MESH,
        )

    def direct(h, b, to, end):
        return (to == end) & (b // r != s)

    def forward(h, p):
        for b, sign, end, send in ((z - h, 1, n - 1, up), (z + h, -1, 0, down)):
            valid = (b >= 0) & (b < n)
            relay = valid
            if h > 0:
                relay = valid & (z != end)

                @pl.when(relay)
                def _():
                    hop(part(xz.at[b], p), b, p, up_sem.at[0, p], z).wait_recv()

            if h < n - 1:
                straight = direct(h, b, z + sign, end)

                @pl.when(valid & (z != end) & ~straight)
                def _():
                    send(h, p).start()

                @pl.when(valid & (z != end) & straight)
                def _():
                    sem = (up_sem if sign == 1 else down_sem).at[h, p]
                    slanted(h, b, p, sem, z + sign).start()

            if h > 0 or sign == 1:
                @pl.when(relay & (b // r != s))
                def _():
                    across(source(h, b, p), b, p).start()

    for p in range(2 * depth):
        forward(0, p)

    zero_row = jnp.zeros((NZ, I), xs.dtype)
    zero_plane = jnp.zeros(xs.shape[2:], xs.dtype)
    for c in range(3):
        xs[0, c] = zero_plane
        xs[planes + 1, c] = zero_plane

        @pl.loop(1, planes + 1)
        def _(q):
            xs[q, c, :NZ, :] = zero_row
            xs[q, c, NZ + cells :, :] = zero_row

    def prepare(ref, u, q, j):
        v = part(ref, u)[...]
        start, size = spans[u // depth]
        rows = lax.broadcasted_iota(jnp.int32, (size, chb), 0) % NZ
        wide = v.astype(jnp.float32)
        before = jnp.where(rows == 0, 0.0, pltpu.roll(wide, 1, 0))
        after = jnp.where(rows == NZ - 1, 0.0, pltpu.roll(wide, size - 1, 0))
        lanes = slice(j * chb, (j + 1) * chb)
        to = slice(NZ + start, NZ + start + size)
        xs[q + 1, 0, to, lanes] = before.astype(xs.dtype)
        xs[q + 1, 1, to, lanes] = v
        xs[q + 1, 2, to, lanes] = after.astype(xs.dtype)

    for half in range(2):
        for h in range(1, n - 1):
            for p in range(depth):
                forward(h, half * depth + p)

    def fetch_half(half):
        for p in range(depth):
            u = half * depth + p
            for j in range(r):
                @pl.when(z == s * r + j)
                def _():
                    prepare(x_ref, u, s * depth + p, j)

                b = s * r + j

                @pl.when(((z == 0) & (b > 0)) | ((z == n - 1) & (b < n - 1)))
                def _():
                    hop(part(xz.at[b], u), b, u, up_sem.at[0, u], z).wait_recv()

                @pl.when(z != s * r + j)
                def _():
                    prepare(xz.at[s * r + j], u, s * depth + p, j)

            @pl.loop(1, S)
            def _(so):
                src = lax.rem(s + so, S)
                for j in range(r):
                    view = part(xr.at[src, j], u)
                    pltpu.make_async_remote_copy(
                        src_ref=view, dst_ref=view,
                        send_sem=a_send.at[0, u], recv_sem=a_recv.at[src, j, u],
                        device_id={"space": src}, device_id_type=MESH,
                    ).wait_recv()
                    prepare(xr.at[src, j], u, src * depth + p, j)

    for t in range(TAPS):
        pltpu.make_async_copy(w_ref.at[t], wv.at[:, t * I : (t + 1) * I], w_sem.at[t]).wait()

    def partial(dest, half):
        window = jnp.concatenate(
            [
                jnp.concatenate(
                    [
                        xs[
                            dest * depth + p + a, c,
                            NZ * b + half * rows_out : NZ * b + (half + 1) * rows_out, :,
                        ]
                        for p in range(depth)
                    ],
                    axis=0,
                )
                for a in range(3)
                for b in range(3)
                for c in range(3)
            ],
            axis=1,
        )
        return lax.dot_general(
            window, wv[...], (((1,), (1,)), ((), ())), preferred_element_type=jnp.float32
        )

    def target(hops, mine):
        far = lax.rem(x + hops, nx)
        return far * 2 + jnp.where(mine == 1, k, 1 - k)

    def half_of(ref, m, half):
        return ref.at[m, half]

    def to_partner(m, half):
        return pltpu.make_async_remote_copy(
            src_ref=half_of(psend, m, half), dst_ref=half_of(precv, m, half),
            send_sem=p_send.at[m, half], recv_sem=p_recv.at[m, half],
            device_id={"space": partner}, device_id_type=MESH,
        )

    def to_chip(m, half, there):
        return pltpu.make_async_remote_copy(
            src_ref=half_of(xsend, m, half), dst_ref=half_of(xrecv, m, half),
            send_sem=q_send.at[m, half], recv_sem=q_recv.at[m, half],
            device_id={"space": there}, device_id_type=MESH,
        )

    def reduce_half(half, first, stop):
        @pl.loop(2 * first, 2 * stop)
        def _(i):
            m = i // 2
            mine = i % 2
            total = partial(target(m + 1, mine), half)

            @pl.when(mine == 0)
            def _():
                psend[m, half] = total
                to_partner(m, half).start()

            @pl.when(mine == 1)
            def _():
                to_partner(m, half).wait_recv()
                if first < nx - 1:
                    xsend[m, half] = total + precv[m, half]
                    to_chip(m, half, target(m + 1, 1)).start()
                else:
                    own[half] = total + precv[m, half]

    fetch_half(0)
    reduce_half(0, 0, nx - 1)
    fetch_half(1)
    reduce_half(1, 0, nx - 1)
    for half in range(2):
        reduce_half(half, nx - 1, nx)

    for half in range(2):
        total = own[half]
        for m in range(nx - 1):
            to_chip(m, half, partner).wait_recv()
            total = total + xrecv[m, half]
        for p in range(depth):
            out_ref[p, half * rows_out : (half + 1) * rows_out, :] = total[
                p * rows_out : (p + 1) * rows_out
            ].astype(out_ref.dtype)

    for h in range(n):
        for p in range(2 * depth):
            if h < n - 1:
                @pl.when((z - h >= 0) & (z < n - 1))
                def _():
                    up(h, p).wait_send()

                @pl.when((z + h < n) & (z > 0))
                def _():
                    down(h, p).wait_send()

            for b, sign, end in ((z - h, 1, n - 1), (z + h, -1, 0)):
                relay = (b >= 0) & (b < n) & (b // r != s)
                if h > 0:
                    relay = relay & ~direct(h - 1, b, z, end)

                if h > 0 or sign == 1:
                    @pl.when(relay)
                    def _():
                        across(source(h, b, p), b, p).wait_send()

    for m in range(nx):
        for half in range(2):
            to_partner(m, half).wait_send()
            if m < nx - 1:
                to_chip(m, half, partner).wait_send()


def general(S, n, fields, conv_weight):
    chb, depth, cells = fields.shape
    owned, I = conv_weight.shape[1:]
    r = I // chb
    nx = S // 2
    planes = S * depth
    bf16, f32 = jnp.bfloat16, jnp.float32
    dma = pltpu.SemaphoreType.DMA
    x = jnp.transpose(fields, (1, 2, 0))
    result = pl.pallas_call(
        functools.partial(general_kernel, S, n, r),
        out_shape=jax.ShapeDtypeStruct((depth, cells, owned), bf16),
        in_specs=[
            pl.BlockSpec(memory_space=pltpu.VMEM),
            pl.BlockSpec(memory_space=pl.ANY),
        ],
        out_specs=pl.BlockSpec(memory_space=pltpu.VMEM),
        scratch_shapes=[
            pltpu.VMEM((n, depth, cells, chb), bf16),
            pltpu.VMEM((S, r, depth, cells, chb), bf16),
            pltpu.VMEM((planes + 2, 3, cells + 2 * NZ, I), bf16),
            pltpu.VMEM((owned, TAPS * I), bf16),
            pltpu.VMEM((nx, 2, depth * cells // 2, owned), f32),
            pltpu.VMEM((nx, 2, depth * cells // 2, owned), f32),
            pltpu.VMEM((nx - 1, 2, depth * cells // 2, owned), f32),
            pltpu.VMEM((nx - 1, 2, depth * cells // 2, owned), f32),
            pltpu.VMEM((2, depth * cells // 2, owned), f32),
            dma((TAPS,)),
            dma((n, 2 * depth)),
            dma((n, 2 * depth)),
            dma((n, 2 * depth)),
            dma((n, 2 * depth)),
            dma((S, r, 2 * depth)),
            dma((nx, 2)),
            dma((nx, 2)),
            dma((nx, 2)),
            dma((nx, 2)),
        ],
        compiler_params=pltpu.CompilerParams(
            collective_id=0, has_side_effects=True, vmem_limit_bytes=62 * 1024 * 1024
        ),
    )(x, conv_weight)
    return jnp.transpose(result, (2, 0, 1))


def solution(mesh):
    return jax.shard_map(
        functools.partial(local, mesh.shape["space"], mesh.shape["chan"]),
        mesh=mesh,
        in_specs=(P("chan", ("groups", "space"), None), P(None, "chan", "space")),
        out_specs=P("chan", ("groups", "space"), None),
        check_vma=False,
    )
```

```python
import functools

import jax
import jax.numpy as jnp
from jax import lax
from jax.experimental import pallas as pl
from jax.experimental.pallas import tpu as pltpu
from jax.sharding import PartitionSpec as P

NZ = 16
TAPS = 27
MESH = pl.DeviceIdType.MESH


PIECES = 4


def plan():
    return [
        ('F', 1, 0, 0),
        ('F', 1, 1, 0),
        ('F', 1, 2, 0),
        ('F', 1, 3, 0),
        ('P', 1, 0),
        ('F', 3, 0, 0),
        ('F', 2, 0, 0),
        ('P', 1, 1),
        ('F', 3, 1, 0),
        ('F', 2, 1, 0),
        ('G', 0),
        ('XA', 0),
        ('F', 3, 2, 0),
        ('F', 2, 2, 0),
        ('G', 1),
        ('XB', 0),
        ('XA', 1),
        ('F', 3, 3, 0),
        ('F', 2, 3, 0),
        ('G', 2),
        ('XB', 1),
        ('XA', 2),
        ('F', 0, 0, 0),
        ('F', 0, 1, 0),
        ('G', 3),
        ('XB', 2),
        ('XA', 3),
        ('F', 0, 2, 0),
        ('F', 0, 3, 0),
        ('P', 0, 0),
        ('XB', 3),
        ('YA', 0),
        ('P', 0, 1),
        ('YA', 1),
        ('YB', 0),
        ('YB', 1),
    ]


def first():
    return [
        ('F', 1, 0),
        ('F', 1, 1),
        ('F', 1, 2),
        ('F', 1, 3),
        ('R', 0),
        ('F', 3, 0),
        ('F', 2, 0),
        ('R', 1),
        ('F', 3, 1),
        ('F', 2, 1),
        ('R', 2),
        ('F', 3, 2),
        ('F', 2, 2),
        ('R', 3),
        ('F', 3, 3),
        ('F', 2, 3),
        ('F', 0, 0),
        ('F', 0, 1),
        ('F', 0, 2),
        ('F', 0, 3),
    ]


def kernel(
    S, n, x_ref, w_ref, out_ref,
    xraw, xloc, xin, xrel, xs, wv, acc, precv, orecv, xsend, xrecv,
    x_sem, w_sem, c_send, r_sem, u_send, d_send, l_send, l_recv, m_send,
    p_send, p_recv, o_send, o_recv, q_send, q_recv,
):
    chb, depth, cells = x_ref.shape
    planes = S * depth
    half = cells // 2
    piece = cells // PIECES
    stops = [0] + [(q + 1) * piece + NZ for q in range(PIECES - 1)] + [cells]
    spans = [(stops[q], stops[q + 1] - stops[q]) for q in range(PIECES)]
    s = lax.axis_index("space")
    z = lax.axis_index("chan")
    x = s // 2
    k = s % 2
    partner = 2 * x + 1 - k
    peer = 2 * (1 - x) + k
    there = 2 * (1 - x) + 1 - k
    source = s == z
    last = ~source & ((z == 0) | (z == n - 1))
    middle = ~source & ~last
    goes_up = (z >= s) & (z < n - 1)
    goes_down = (z <= s) & (z > 0)
    edge = (s == 0) | (s == n - 1)
    far_up = goes_up & (source | ~edge)
    far_down = goes_down & (source | ~edge)
    ahead = jnp.where(x == 1, 1, -1)
    origin = jnp.where(x == 1, 0, n - 1)
    feeds = z == origin
    relays = z == origin + 2 * ahead
    away = jnp.where(s == 0, z - s, s - z)

    pltpu.make_async_copy(x_ref, xraw, x_sem).start()

    barrier = pltpu.get_barrier_semaphore()

    def greet(space, chan):
        pl.semaphore_signal(
            barrier, inc=1, device_id={"space": space, "chan": chan}, device_id_type=MESH
        )

    greet(partner, z)
    greet(peer, z)

    @pl.when(z > s)
    def _():
        greet(s, z - 1)

    @pl.when(z < s)
    def _():
        greet(s, z + 1)

    @pl.when(source)
    def _():
        for so in range(1, S):
            greet(lax.rem(s + so, S), z)

    @pl.when(relays)
    def _():
        greet(s, origin)

    @pl.when(edge & (away >= 2))
    def _():
        row = jnp.where(s == 0, 2, n - 3)
        for j in range(2):
            greet(2 * (1 - x) + j, row)

    for t in range(TAPS):
        pltpu.make_async_copy(w_ref.at[t], wv.at[:, t * chb : (t + 1) * chb], w_sem.at[t]).start()

    pltpu.make_async_copy(x_ref, xraw, x_sem).wait()
    own = pltpu.einshape("cpm->pmc", xraw[...])
    xloc[...] = own

    @pl.when(source)
    def _():
        xin[s] = own

    def one(flag):
        return jnp.where(flag, 1, 0)

    pl.semaphore_wait(
        barrier,
        2 + one(~source) + one(goes_up) + one(goes_down) + one(feeds) + 2 * one(relays),
    )

    def part(ref, p, q):
        return ref.at[p, pl.ds(*spans[q])]

    def gather(p, q):
        return pltpu.make_async_remote_copy(
            src_ref=part(xloc, p, q), dst_ref=part(xin.at[s], p, q), send_sem=c_send.at[p, q],
            recv_sem=r_sem.at[s, p, q], device_id={"space": z}, device_id_type=MESH,
        )

    def feed(p, q):
        return pltpu.make_async_remote_copy(
            src_ref=part(xloc, p, q), dst_ref=part(xrel, p, q), send_sem=l_send.at[p, q],
            recv_sem=l_recv.at[p, q], device_id={"chan": z + 2 * ahead}, device_id_type=MESH,
        )

    def relay(j, p, q):
        return pltpu.make_async_remote_copy(
            src_ref=part(xrel, p, q), dst_ref=part(xin.at[s], p, q), send_sem=m_send.at[j, p, q],
            recv_sem=r_sem.at[s, p, q], device_id={"space": origin, "chan": z + j * ahead},
            device_id_type=MESH,
        )

    def lane(b, p, q, sem, to):
        view = part(xin.at[b], p, q)
        return pltpu.make_async_remote_copy(
            src_ref=view, dst_ref=view, send_sem=sem.at[b, p, q], recv_sem=r_sem.at[b, p, q],
            device_id={"chan": to}, device_id_type=MESH,
        )

    def block(o):
        return jnp.where(x == 0, o, S - 1 - o)

    for q in range(PIECES):
        for p in range(depth):
            @pl.when(feeds)
            def _():
                feed(p, q).start()

            @pl.when(~source)
            def _():
                gather(p, q).start()

    def fetch(o, q):
        b = block(o)
        for p in range(depth):
            @pl.when(b != jnp.where(source, s, S))
            def _():
                lane(b, p, q, u_send, lax.rem(z + 1, n)).wait_recv()

            @pl.when(far_up if o >= 2 else goes_up)
            def _():
                lane(b, p, q, u_send, z + 1).start()

            @pl.when(far_down if o >= 2 else goes_down)
            def _():
                lane(b, p, q, d_send, z - 1).start()

    def pass_piece(q):
        for p in range(depth):
            feed(p, q).wait_recv()
            for j in (1, 0):
                relay(j, p, q).start()

    def shifted(b, start, size):
        rows = lax.broadcasted_iota(jnp.int32, (size, chb), 0) % NZ
        to = slice(NZ + start, NZ + start + size)
        for p in range(depth):
            v = xin[b, p, start : start + size, :]
            wide = v.astype(jnp.float32)
            before = jnp.where(rows == 0, 0.0, pltpu.roll(wide, 1, 0))
            after = jnp.where(rows == NZ - 1, 0.0, pltpu.roll(wide, size - 1, 0))
            at = b * depth + p
            xs[at, 0, to, :] = before.astype(xs.dtype)
            xs[at, 1, to, :] = v
            xs[at, 2, to, :] = after.astype(xs.dtype)

    def multiply(base, count, start, size):
        window = jnp.concatenate(
            [
                jnp.concatenate(
                    [xs[base + p, c, NZ * y + start : NZ * y + start + size, :] for p in range(count)],
                    axis=0,
                )
                for y in range(3)
                for c in range(3)
            ],
            axis=1,
        )
        for a in range(3):
            terms = lax.dot_general(
                window, wv[:, a * 9 * chb : (a + 1) * 9 * chb], (((1,), (1,)), ((), ())),
                preferred_element_type=jnp.float32,
            )
            acc[pl.ds(base + 2 - a, count), start : start + size, :] += terms.reshape(
                count, size, chb
            )

    def near(o, h):
        b = block(o)
        start = 0 if h == 0 else stops[PIECES // 2]
        stop = stops[PIECES // 2] if h == 0 else cells
        shifted(b, start, stop - start)
        multiply(b * depth, depth, h * half, half)

    def distant(q):
        for o in (3, 2):
            shifted(block(o), *spans[q])
        multiply(2 * (1 - x) * depth, 2 * depth, q * piece, piece)

    def sums(core, start, size):
        return acc.at[pl.ds(core * depth + 1, depth), start : start + size]

    def far_piece(q):
        return pltpu.make_async_remote_copy(
            src_ref=sums(there, q * piece, piece), dst_ref=precv.at[q],
            send_sem=p_send.at[q], recv_sem=p_recv.at[q],
            device_id={"space": partner}, device_id_type=MESH,
        )

    def own_half(h):
        return pltpu.make_async_remote_copy(
            src_ref=sums(partner, h * half, half), dst_ref=orecv.at[h],
            send_sem=o_send.at[h], recv_sem=o_recv.at[h],
            device_id={"space": partner}, device_id_type=MESH,
        )

    def across(q):
        return pltpu.make_async_remote_copy(
            src_ref=xsend.at[q], dst_ref=xrecv.at[q], send_sem=q_send.at[q], recv_sem=q_recv.at[q],
            device_id={"space": peer}, device_id_type=MESH,
        )

    def pass_on(q):
        far_piece(q).wait_recv()
        xsend[q] = sums(peer, q * piece, piece)[...] + precv[q]
        across(q).start()

    def finish(h):
        own_half(h).wait_recv()
        total = sums(s, h * half, half)[...] + orecv[h]
        for j in range(PIECES // 2):
            across(h * PIECES // 2 + j).wait_recv()
        far = jnp.concatenate([xrecv[h * PIECES // 2 + j] for j in range(PIECES // 2)], axis=1)
        total = total + far
        wide = jnp.concatenate([total[p].T for p in range(depth)], axis=1)
        out_ref[:, :, h * half : (h + 1) * half] = wide.reshape(chb, depth, half).astype(
            out_ref.dtype
        )

    @pl.when(source)
    def _():
        for op in first():
            if op[0] == "F":
                fetch(*op[1:])
            else:
                @pl.when(relays)
                def _():
                    pass_piece(op[1])

    zero_row = jnp.zeros((NZ, chb), xs.dtype)
    for at in range(planes):
        for c in range(3):
            xs[at, c, :NZ, :] = zero_row
            xs[at, c, NZ + cells :, :] = zero_row
    for at in range(planes + 2):
        acc[at] = jnp.zeros(acc.shape[1:], acc.dtype)

    ready = False
    for op in plan():
        if op[0] == "F":
            @pl.when(middle)
            def _():
                fetch(op[1], op[2])
                if op[1] == 3:
                    @pl.when(relays)
                    def _():
                        pass_piece(op[2])
        if op[0] in ("P", "G"):
            needed = (
                [(op[1], 2 * op[2]), (op[1], 2 * op[2] + 1)] if op[0] == "P"
                else [(3, op[1]), (2, op[1])]
            )

            @pl.when(last)
            def _():
                for o, q in needed:
                    for p in range(depth):
                        lane(block(o), p, q, u_send, lax.rem(z + 1, n)).wait_recv()

        if op[0] in ("P", "G") and not ready:
            ready = True
            for t in range(TAPS):
                pltpu.make_async_copy(
                    w_ref.at[t], wv.at[:, t * chb : (t + 1) * chb], w_sem.at[t]
                ).wait()
        if op[0] == "P":
            near(*op[1:])
        if op[0] == "G":
            distant(op[1])
        if op[0] == "XA":
            far_piece(op[1]).start()
        if op[0] == "XB":
            pass_on(op[1])
        if op[0] == "YA":
            own_half(op[1]).start()
        if op[0] == "YB":
            finish(op[1])

    for q in range(PIECES):
        for p in range(depth):
            @pl.when(feeds)
            def _():
                feed(p, q).wait_send()

            @pl.when(~source)
            def _():
                gather(p, q).wait_send()

            @pl.when(relays)
            def _():
                for j in range(2):
                    relay(j, p, q).wait_send()

            for o in range(S):
                @pl.when(far_up if o >= 2 else goes_up)
                def _():
                    lane(block(o), p, q, u_send, lax.rem(z + 1, n)).wait_send()

                @pl.when(far_down if o >= 2 else goes_down)
                def _():
                    lane(block(o), p, q, d_send, lax.rem(z + n - 1, n)).wait_send()

        far_piece(q).wait_send()
        across(q).wait_send()
    for h in range(2):
        own_half(h).wait_send()


def local(S, n, fields, conv_weight):
    chb, depth, cells = fields.shape
    owned, I = conv_weight.shape[1:]
    if not (S == n == 4 and owned == I == chb):
        return general(S, n, fields, conv_weight)
    planes = S * depth
    bf16, f32 = jnp.bfloat16, jnp.float32
    dma = pltpu.SemaphoreType.DMA
    piece = cells // PIECES
    return pl.pallas_call(
        functools.partial(kernel, S, n),
        out_shape=pltpu.VMEM((owned, depth, cells), bf16),
        in_specs=[pl.BlockSpec(memory_space=pl.ANY), pl.BlockSpec(memory_space=pl.ANY)],
        out_specs=pl.BlockSpec(memory_space=pltpu.VMEM),
        scratch_shapes=[
            pltpu.VMEM((chb, depth, cells), bf16),
            pltpu.VMEM((depth, cells, chb), bf16),
            pltpu.VMEM((S, depth, cells, chb), bf16),
            pltpu.VMEM((depth, cells, chb), bf16),
            pltpu.VMEM((planes, 3, cells + 2 * NZ, chb), bf16),
            pltpu.VMEM((owned, TAPS * chb), bf16),
            pltpu.VMEM((planes + 2, cells, owned), f32),
            pltpu.VMEM((PIECES, depth, piece, owned), f32),
            pltpu.VMEM((2, depth, cells // 2, owned), f32),
            pltpu.VMEM((PIECES, depth, piece, owned), f32),
            pltpu.VMEM((PIECES, depth, piece, owned), f32),
            dma(()),
            dma((TAPS,)),
            dma((depth, PIECES)),
            dma((S, depth, PIECES)),
            dma((S, depth, PIECES)),
            dma((S, depth, PIECES)),
            dma((depth, PIECES)),
            dma((depth, PIECES)),
            dma((2, depth, PIECES)),
            dma((PIECES,)),
            dma((PIECES,)),
            dma((2,)),
            dma((2,)),
            dma((PIECES,)),
            dma((PIECES,)),
        ],
        compiler_params=pltpu.CompilerParams(
            collective_id=0, has_side_effects=True, vmem_limit_bytes=62 * 1024 * 1024
        ),
    )(fields, conv_weight)


def general_kernel(
    S, n, r, x_ref, w_ref, out_ref,
    xz, xr, xs, wv, psend, precv, xsend, xrecv, own,
    w_sem, up_sem, down_sem, z_sem, a_send, a_recv, p_send, p_recv, q_send, q_recv,
):
    depth, cells, chb = x_ref.shape
    I = r * chb
    nx = S // 2
    planes = S * depth
    s = lax.axis_index("space")
    z = lax.axis_index("chan")
    x = s // 2
    k = s % 2
    partner = x * 2 + (1 - k)

    for t in range(TAPS):
        pltpu.make_async_copy(w_ref.at[t], wv.at[:, t * I : (t + 1) * I], w_sem.at[t]).start()

    barrier = pltpu.get_barrier_semaphore()

    for so in range(S):
        for step, there in ((-1, z > 0), (1, z < n - 1)):
            @pl.when(there)
            def _():
                pl.semaphore_signal(
                    barrier, inc=1, device_id={"space": lax.rem(s + so, S), "chan": z + step},
                    device_id_type=MESH,
                )

    for so in range(1, S):
        pl.semaphore_signal(
            barrier, inc=1, device_id={"space": lax.rem(s + so, S)}, device_id_type=MESH
        )
    here = jnp.where(z > 0, S, 0) + jnp.where(z < n - 1, S, 0) + (S - 1)
    pl.semaphore_wait(barrier, here)

    split = cells // 2 + NZ
    spans = ((0, split), (split, cells - split))
    rows_out = cells // 2

    def part(ref, u):
        return ref.at[u % depth, pl.ds(*spans[u // depth])]

    def hop(src, b, p, sem, to):
        return pltpu.make_async_remote_copy(
            src_ref=src, dst_ref=part(xz.at[b], p), send_sem=sem, recv_sem=z_sem.at[b, p],
            device_id={"chan": to}, device_id_type=MESH,
        )

    def across(src, b, p):
        return pltpu.make_async_remote_copy(
            src_ref=src, dst_ref=part(xr.at[s, b % r], p), send_sem=a_send.at[b, p],
            recv_sem=a_recv.at[s, b % r, p],
            device_id={"space": b // r}, device_id_type=MESH,
        )

    def source(h, b, p):
        return part(x_ref, p) if h == 0 else part(xz.at[b], p)

    def up(h, p):
        return hop(source(h, z - h, p), z - h, p, up_sem.at[h, p], z + 1)

    def down(h, p):
        return hop(source(h, z + h, p), z + h, p, down_sem.at[h, p], z - 1)

    def slanted(h, b, p, sem, to):
        return pltpu.make_async_remote_copy(
            src_ref=source(h, b, p), dst_ref=part(xr.at[s, b % r], p), send_sem=sem,
            recv_sem=a_recv.at[s, b % r, p],
            device_id={"space": b // r, "chan": to}, device_id_type=MESH,
        )

    def direct(h, b, to, end):
        return (to == end) & (b // r != s)

    def forward(h, p):
        for b, sign, end, send in ((z - h, 1, n - 1, up), (z + h, -1, 0, down)):
            valid = (b >= 0) & (b < n)
            relay = valid
            if h > 0:
                relay = valid & (z != end)

                @pl.when(relay)
                def _():
                    hop(part(xz.at[b], p), b, p, up_sem.at[0, p], z).wait_recv()

            if h < n - 1:
                straight = direct(h, b, z + sign, end)

                @pl.when(valid & (z != end) & ~straight)
                def _():
                    send(h, p).start()

                @pl.when(valid & (z != end) & straight)
                def _():
                    sem = (up_sem if sign == 1 else down_sem).at[h, p]
                    slanted(h, b, p, sem, z + sign).start()

            if h > 0 or sign == 1:
                @pl.when(relay & (b // r != s))
                def _():
                    across(source(h, b, p), b, p).start()

    for p in range(2 * depth):
        forward(0, p)

    zero_row = jnp.zeros((NZ, I), xs.dtype)
    zero_plane = jnp.zeros(xs.shape[2:], xs.dtype)
    for c in range(3):
        xs[0, c] = zero_plane
        xs[planes + 1, c] = zero_plane

        @pl.loop(1, planes + 1)
        def _(q):
            xs[q, c, :NZ, :] = zero_row
            xs[q, c, NZ + cells :, :] = zero_row

    def prepare(ref, u, q, j):
        v = part(ref, u)[...]
        start, size = spans[u // depth]
        rows = lax.broadcasted_iota(jnp.int32, (size, chb), 0) % NZ
        wide = v.astype(jnp.float32)
        before = jnp.where(rows == 0, 0.0, pltpu.roll(wide, 1, 0))
        after = jnp.where(rows == NZ - 1, 0.0, pltpu.roll(wide, size - 1, 0))
        lanes = slice(j * chb, (j + 1) * chb)
        to = slice(NZ + start, NZ + start + size)
        xs[q + 1, 0, to, lanes] = before.astype(xs.dtype)
        xs[q + 1, 1, to, lanes] = v
        xs[q + 1, 2, to, lanes] = after.astype(xs.dtype)

    for half in range(2):
        for h in range(1, n - 1):
            for p in range(depth):
                forward(h, half * depth + p)

    def fetch_half(half):
        for p in range(depth):
            u = half * depth + p
            for j in range(r):
                @pl.when(z == s * r + j)
                def _():
                    prepare(x_ref, u, s * depth + p, j)

                b = s * r + j

                @pl.when(((z == 0) & (b > 0)) | ((z == n - 1) & (b < n - 1)))
                def _():
                    hop(part(xz.at[b], u), b, u, up_sem.at[0, u], z).wait_recv()

                @pl.when(z != s * r + j)
                def _():
                    prepare(xz.at[s * r + j], u, s * depth + p, j)

            @pl.loop(1, S)
            def _(so):
                src = lax.rem(s + so, S)
                for j in range(r):
                    view = part(xr.at[src, j], u)
                    pltpu.make_async_remote_copy(
                        src_ref=view, dst_ref=view,
                        send_sem=a_send.at[0, u], recv_sem=a_recv.at[src, j, u],
                        device_id={"space": src}, device_id_type=MESH,
                    ).wait_recv()
                    prepare(xr.at[src, j], u, src * depth + p, j)

    for t in range(TAPS):
        pltpu.make_async_copy(w_ref.at[t], wv.at[:, t * I : (t + 1) * I], w_sem.at[t]).wait()

    def partial(dest, half):
        window = jnp.concatenate(
            [
                jnp.concatenate(
                    [
                        xs[
                            dest * depth + p + a, c,
                            NZ * b + half * rows_out : NZ * b + (half + 1) * rows_out, :,
                        ]
                        for p in range(depth)
                    ],
                    axis=0,
                )
                for a in range(3)
                for b in range(3)
                for c in range(3)
            ],
            axis=1,
        )
        return lax.dot_general(
            window, wv[...], (((1,), (1,)), ((), ())), preferred_element_type=jnp.float32
        )

    def target(hops, mine):
        far = lax.rem(x + hops, nx)
        return far * 2 + jnp.where(mine == 1, k, 1 - k)

    def half_of(ref, m, half):
        return ref.at[m, half]

    def to_partner(m, half):
        return pltpu.make_async_remote_copy(
            src_ref=half_of(psend, m, half), dst_ref=half_of(precv, m, half),
            send_sem=p_send.at[m, half], recv_sem=p_recv.at[m, half],
            device_id={"space": partner}, device_id_type=MESH,
        )

    def to_chip(m, half, there):
        return pltpu.make_async_remote_copy(
            src_ref=half_of(xsend, m, half), dst_ref=half_of(xrecv, m, half),
            send_sem=q_send.at[m, half], recv_sem=q_recv.at[m, half],
            device_id={"space": there}, device_id_type=MESH,
        )

    def reduce_half(half, first, stop):
        @pl.loop(2 * first, 2 * stop)
        def _(i):
            m = i // 2
            mine = i % 2
            total = partial(target(m + 1, mine), half)

            @pl.when(mine == 0)
            def _():
                psend[m, half] = total
                to_partner(m, half).start()

            @pl.when(mine == 1)
            def _():
                to_partner(m, half).wait_recv()
                if first < nx - 1:
                    xsend[m, half] = total + precv[m, half]
                    to_chip(m, half, target(m + 1, 1)).start()
                else:
                    own[half] = total + precv[m, half]

    fetch_half(0)
    reduce_half(0, 0, nx - 1)
    fetch_half(1)
    reduce_half(1, 0, nx - 1)
    for half in range(2):
        reduce_half(half, nx - 1, nx)

    for half in range(2):
        total = own[half]
        for m in range(nx - 1):
            to_chip(m, half, partner).wait_recv()
            total = total + xrecv[m, half]
        for p in range(depth):
            out_ref[p, half * rows_out : (half + 1) * rows_out, :] = total[
                p * rows_out : (p + 1) * rows_out
            ].astype(out_ref.dtype)

    for h in range(n):
        for p in range(2 * depth):
            if h < n - 1:
                @pl.when((z - h >= 0) & (z < n - 1))
                def _():
                    up(h, p).wait_send()

                @pl.when((z + h < n) & (z > 0))
                def _():
                    down(h, p).wait_send()

            for b, sign, end in ((z - h, 1, n - 1), (z + h, -1, 0)):
                relay = (b >= 0) & (b < n) & (b // r != s)
                if h > 0:
                    relay = relay & ~direct(h - 1, b, z, end)

                if h > 0 or sign == 1:
                    @pl.when(relay)
                    def _():
                        across(source(h, b, p), b, p).wait_send()

    for m in range(nx):
        for half in range(2):
            to_partner(m, half).wait_send()
            if m < nx - 1:
                to_chip(m, half, partner).wait_send()


def general(S, n, fields, conv_weight):
    chb, depth, cells = fields.shape
    owned, I = conv_weight.shape[1:]
    r = I // chb
    nx = S // 2
    planes = S * depth
    bf16, f32 = jnp.bfloat16, jnp.float32
    dma = pltpu.SemaphoreType.DMA
    x = jnp.transpose(fields, (1, 2, 0))
    result = pl.pallas_call(
        functools.partial(general_kernel, S, n, r),
        out_shape=jax.ShapeDtypeStruct((depth, cells, owned), bf16),
        in_specs=[
            pl.BlockSpec(memory_space=pltpu.VMEM),
            pl.BlockSpec(memory_space=pl.ANY),
        ],
        out_specs=pl.BlockSpec(memory_space=pltpu.VMEM),
        scratch_shapes=[
            pltpu.VMEM((n, depth, cells, chb), bf16),
            pltpu.VMEM((S, r, depth, cells, chb), bf16),
            pltpu.VMEM((planes + 2, 3, cells + 2 * NZ, I), bf16),
            pltpu.VMEM((owned, TAPS * I), bf16),
            pltpu.VMEM((nx, 2, depth * cells // 2, owned), f32),
            pltpu.VMEM((nx, 2, depth * cells // 2, owned), f32),
            pltpu.VMEM((nx - 1, 2, depth * cells // 2, owned), f32),
            pltpu.VMEM((nx - 1, 2, depth * cells // 2, owned), f32),
            pltpu.VMEM((2, depth * cells // 2, owned), f32),
            dma((TAPS,)),
            dma((n, 2 * depth)),
            dma((n, 2 * depth)),
            dma((n, 2 * depth)),
            dma((n, 2 * depth)),
            dma((S, r, 2 * depth)),
            dma((nx, 2)),
            dma((nx, 2)),
            dma((nx, 2)),
            dma((nx, 2)),
        ],
        compiler_params=pltpu.CompilerParams(
            collective_id=0, has_side_effects=True, vmem_limit_bytes=62 * 1024 * 1024
        ),
    )(x, conv_weight)
    return jnp.transpose(result, (2, 0, 1))


def solution(mesh):
    return jax.shard_map(
        functools.partial(local, mesh.shape["space"], mesh.shape["chan"]),
        mesh=mesh,
        in_specs=(P("chan", ("groups", "space"), None), P(None, "chan", "space")),
        out_specs=P("chan", ("groups", "space"), None),
        check_vma=False,
    )
```

```python
import functools

import jax
import jax.numpy as jnp
from jax import lax
from jax.experimental import pallas as pl
from jax.experimental.pallas import tpu as pltpu
from jax.sharding import PartitionSpec as P

NZ = 16
TAPS = 27
MESH = pl.DeviceIdType.MESH


PIECES = 4


def plan():
    return [
        ('F', 1, 0, 0),
        ('F', 1, 1, 0),
        ('F', 1, 2, 0),
        ('F', 1, 3, 0),
        ('P', 1, 0),
        ('F', 3, 0, 0),
        ('F', 2, 0, 0),
        ('P', 1, 1),
        ('F', 3, 1, 0),
        ('F', 2, 1, 0),
        ('G', 0),
        ('XA', 0),
        ('F', 3, 2, 0),
        ('F', 2, 2, 0),
        ('G', 1),
        ('XB', 0),
        ('XA', 1),
        ('F', 3, 3, 0),
        ('F', 2, 3, 0),
        ('G', 2),
        ('XB', 1),
        ('XA', 2),
        ('F', 0, 0, 0),
        ('F', 0, 1, 0),
        ('G', 3),
        ('XB', 2),
        ('XA', 3),
        ('F', 0, 2, 0),
        ('P', 0, 0),
        ('XB', 3),
        ('YA', 0),
        ('F', 0, 3, 0),
        ('Q', 0, 2),
        ('Q', 0, 3),
        ('YA', 1),
        ('YB', 0),
        ('YB', 1),
    ]


def first():
    return [
        ('F', 1, 0),
        ('F', 1, 1),
        ('F', 1, 2),
        ('F', 1, 3),
        ('R', 0),
        ('F', 3, 0),
        ('F', 2, 0),
        ('R', 1),
        ('F', 3, 1),
        ('F', 2, 1),
        ('R', 2),
        ('F', 3, 2),
        ('F', 2, 2),
        ('R', 3),
        ('F', 3, 3),
        ('F', 2, 3),
        ('F', 0, 0),
        ('F', 0, 1),
        ('F', 0, 2),
        ('F', 0, 3),
    ]


def kernel(
    S, n, x_ref, w_ref, out_ref,
    xraw, xloc, xin, xrel, xs, wv, acc, precv, orecv, xsend, xrecv,
    x_sem, w_sem, c_send, r_sem, u_send, d_send, l_send, l_recv, m_send,
    p_send, p_recv, o_send, o_recv, q_send, q_recv,
):
    chb, depth, cells = x_ref.shape
    planes = S * depth
    half = cells // 2
    piece = cells // PIECES
    stops = [0] + [(q + 1) * piece + NZ for q in range(PIECES - 1)] + [cells]
    spans = [(stops[q], stops[q + 1] - stops[q]) for q in range(PIECES)]
    s = lax.axis_index("space")
    z = lax.axis_index("chan")
    x = s // 2
    k = s % 2
    partner = 2 * x + 1 - k
    peer = 2 * (1 - x) + k
    there = 2 * (1 - x) + 1 - k
    source = s == z
    last = ~source & ((z == 0) | (z == n - 1))
    middle = ~source & ~last
    goes_up = (z >= s) & (z < n - 1)
    goes_down = (z <= s) & (z > 0)
    edge = (s == 0) | (s == n - 1)
    far_up = goes_up & (source | ~edge)
    far_down = goes_down & (source | ~edge)
    ahead = jnp.where(x == 1, 1, -1)
    origin = jnp.where(x == 1, 0, n - 1)
    feeds = z == origin
    relays = z == origin + 2 * ahead
    away = jnp.where(s == 0, z - s, s - z)

    pltpu.make_async_copy(x_ref, xraw, x_sem).start()

    barrier = pltpu.get_barrier_semaphore()

    def greet(space, chan):
        pl.semaphore_signal(
            barrier, inc=1, device_id={"space": space, "chan": chan}, device_id_type=MESH
        )

    greet(partner, z)
    greet(peer, z)

    @pl.when(z > s)
    def _():
        greet(s, z - 1)

    @pl.when(z < s)
    def _():
        greet(s, z + 1)

    @pl.when(source)
    def _():
        for so in range(1, S):
            greet(lax.rem(s + so, S), z)

    @pl.when(relays)
    def _():
        greet(s, origin)

    @pl.when(edge & (away >= 2))
    def _():
        row = jnp.where(s == 0, 2, n - 3)
        for j in range(2):
            greet(2 * (1 - x) + j, row)

    for t in range(TAPS):
        pltpu.make_async_copy(w_ref.at[t], wv.at[:, t * chb : (t + 1) * chb], w_sem.at[t]).start()

    pltpu.make_async_copy(x_ref, xraw, x_sem).wait()
    own = pltpu.einshape("cpm->pmc", xraw[...])
    xloc[...] = own

    @pl.when(source)
    def _():
        xin[s] = own

    def one(flag):
        return jnp.where(flag, 1, 0)

    pl.semaphore_wait(
        barrier,
        2 + one(~source) + one(goes_up) + one(goes_down) + one(feeds) + 2 * one(relays),
    )

    def part(ref, p, q):
        return ref.at[p, pl.ds(*spans[q])]

    def gather(p, q):
        return pltpu.make_async_remote_copy(
            src_ref=part(xloc, p, q), dst_ref=part(xin.at[s], p, q), send_sem=c_send.at[p, q],
            recv_sem=r_sem.at[s, p, q], device_id={"space": z}, device_id_type=MESH,
        )

    def feed(p, q):
        return pltpu.make_async_remote_copy(
            src_ref=part(xloc, p, q), dst_ref=part(xrel, p, q), send_sem=l_send.at[p, q],
            recv_sem=l_recv.at[p, q], device_id={"chan": z + 2 * ahead}, device_id_type=MESH,
        )

    def relay(j, p, q):
        return pltpu.make_async_remote_copy(
            src_ref=part(xrel, p, q), dst_ref=part(xin.at[s], p, q), send_sem=m_send.at[j, p, q],
            recv_sem=r_sem.at[s, p, q], device_id={"space": origin, "chan": z + j * ahead},
            device_id_type=MESH,
        )

    def lane(b, p, q, sem, to):
        view = part(xin.at[b], p, q)
        return pltpu.make_async_remote_copy(
            src_ref=view, dst_ref=view, send_sem=sem.at[b, p, q], recv_sem=r_sem.at[b, p, q],
            device_id={"chan": to}, device_id_type=MESH,
        )

    def block(o):
        return jnp.where(x == 0, o, S - 1 - o)

    for q in range(PIECES):
        for p in range(depth):
            @pl.when(~source)
            def _():
                gather(p, q).start()

            @pl.when(feeds)
            def _():
                feed(p, q).start()

    def fetch(o, q):
        b = block(o)
        for p in range(depth):
            @pl.when(b != jnp.where(source, s, S))
            def _():
                lane(b, p, q, u_send, lax.rem(z + 1, n)).wait_recv()

            @pl.when(far_up if o >= 2 else goes_up)
            def _():
                lane(b, p, q, u_send, z + 1).start()

            @pl.when(far_down if o >= 2 else goes_down)
            def _():
                lane(b, p, q, d_send, z - 1).start()

    def pass_piece(q):
        for p in range(depth):
            feed(p, q).wait_recv()
            for j in (1, 0):
                relay(j, p, q).start()

    def shifted(b, start, size):
        rows = lax.broadcasted_iota(jnp.int32, (size, chb), 0) % NZ
        to = slice(NZ + start, NZ + start + size)
        for p in range(depth):
            v = xin[b, p, start : start + size, :]
            wide = v.astype(jnp.float32)
            before = jnp.where(rows == 0, 0.0, pltpu.roll(wide, 1, 0))
            after = jnp.where(rows == NZ - 1, 0.0, pltpu.roll(wide, size - 1, 0))
            at = b * depth + p
            xs[at, 0, to, :] = before.astype(xs.dtype)
            xs[at, 1, to, :] = v
            xs[at, 2, to, :] = after.astype(xs.dtype)

    def multiply(base, count, start, size):
        window = jnp.concatenate(
            [
                jnp.concatenate(
                    [xs[base + p, c, NZ * y + start : NZ * y + start + size, :] for p in range(count)],
                    axis=0,
                )
                for y in range(3)
                for c in range(3)
            ],
            axis=1,
        )
        for a in range(3):
            terms = lax.dot_general(
                window, wv[:, a * 9 * chb : (a + 1) * 9 * chb], (((1,), (1,)), ((), ())),
                preferred_element_type=jnp.float32,
            )
            acc[pl.ds(base + 2 - a, count), start : start + size, :] += terms.reshape(
                count, size, chb
            )

    def near(o, h):
        b = block(o)
        start = 0 if h == 0 else stops[PIECES // 2]
        stop = stops[PIECES // 2] if h == 0 else cells
        shifted(b, start, stop - start)
        multiply(b * depth, depth, h * half, half)

    def distant(q):
        for o in (3, 2):
            shifted(block(o), *spans[q])
        multiply(2 * (1 - x) * depth, 2 * depth, q * piece, piece)

    def sums(core, start, size):
        return acc.at[pl.ds(core * depth + 1, depth), start : start + size]

    def far_piece(q):
        return pltpu.make_async_remote_copy(
            src_ref=sums(there, q * piece, piece), dst_ref=precv.at[q],
            send_sem=p_send.at[q], recv_sem=p_recv.at[q],
            device_id={"space": partner}, device_id_type=MESH,
        )

    def own_half(h):
        return pltpu.make_async_remote_copy(
            src_ref=sums(partner, h * half, half), dst_ref=orecv.at[h],
            send_sem=o_send.at[h], recv_sem=o_recv.at[h],
            device_id={"space": partner}, device_id_type=MESH,
        )

    def across(q):
        return pltpu.make_async_remote_copy(
            src_ref=xsend.at[q], dst_ref=xrecv.at[q], send_sem=q_send.at[q], recv_sem=q_recv.at[q],
            device_id={"space": peer}, device_id_type=MESH,
        )

    def pass_on(q):
        far_piece(q).wait_recv()
        xsend[q] = sums(peer, q * piece, piece)[...] + precv[q]
        across(q).start()

    def finish(h):
        own_half(h).wait_recv()
        total = sums(s, h * half, half)[...] + orecv[h]
        for j in range(PIECES // 2):
            across(h * PIECES // 2 + j).wait_recv()
        far = jnp.concatenate([xrecv[h * PIECES // 2 + j] for j in range(PIECES // 2)], axis=1)
        total = total + far
        wide = jnp.concatenate([total[p].T for p in range(depth)], axis=1)
        out_ref[:, :, h * half : (h + 1) * half] = wide.reshape(chb, depth, half).astype(
            out_ref.dtype
        )

    @pl.when(source)
    def _():
        for op in first():
            if op[0] == "F":
                fetch(*op[1:])
            else:
                @pl.when(relays)
                def _():
                    pass_piece(op[1])

    zero_row = jnp.zeros((NZ, chb), xs.dtype)
    for at in range(planes):
        for c in range(3):
            xs[at, c, :NZ, :] = zero_row
            xs[at, c, NZ + cells :, :] = zero_row
    for at in range(planes + 2):
        acc[at] = jnp.zeros(acc.shape[1:], acc.dtype)

    ready = False
    for op in plan():
        if op[0] == "F":
            @pl.when(middle)
            def _():
                fetch(op[1], op[2])
                if op[1] == 3:
                    @pl.when(relays)
                    def _():
                        pass_piece(op[2])
        if op[0] in ("P", "G", "Q"):
            needed = [op[1:3]] if op[0] == "Q" else (
                [(op[1], 2 * op[2]), (op[1], 2 * op[2] + 1)] if op[0] == "P"
                else [(3, op[1]), (2, op[1])]
            )

            @pl.when(last)
            def _():
                for o, q in needed:
                    for p in range(depth):
                        lane(block(o), p, q, u_send, lax.rem(z + 1, n)).wait_recv()

        if op[0] in ("P", "G") and not ready:
            ready = True
            for t in range(TAPS):
                pltpu.make_async_copy(
                    w_ref.at[t], wv.at[:, t * chb : (t + 1) * chb], w_sem.at[t]
                ).wait()
        if op[0] == "P":
            near(*op[1:])
        if op[0] == "G":
            distant(op[1])
        if op[0] == "Q":
            b = block(op[1])
            shifted(b, *spans[op[2]])
            multiply(b * depth, depth, op[2] * piece, piece)
        if op[0] == "XA":
            far_piece(op[1]).start()
        if op[0] == "XB":
            pass_on(op[1])
        if op[0] == "YA":
            own_half(op[1]).start()
        if op[0] == "YB":
            finish(op[1])

    for q in range(PIECES):
        for p in range(depth):
            @pl.when(feeds)
            def _():
                feed(p, q).wait_send()

            @pl.when(~source)
            def _():
                gather(p, q).wait_send()

            @pl.when(relays)
            def _():
                for j in range(2):
                    relay(j, p, q).wait_send()

            for o in range(S):
                @pl.when(far_up if o >= 2 else goes_up)
                def _():
                    lane(block(o), p, q, u_send, lax.rem(z + 1, n)).wait_send()

                @pl.when(far_down if o >= 2 else goes_down)
                def _():
                    lane(block(o), p, q, d_send, lax.rem(z + n - 1, n)).wait_send()

        far_piece(q).wait_send()
        across(q).wait_send()
    for h in range(2):
        own_half(h).wait_send()


def local(S, n, fields, conv_weight):
    chb, depth, cells = fields.shape
    owned, I = conv_weight.shape[1:]
    if not (S == n == 4 and owned == I == chb):
        return general(S, n, fields, conv_weight)
    planes = S * depth
    bf16, f32 = jnp.bfloat16, jnp.float32
    dma = pltpu.SemaphoreType.DMA
    piece = cells // PIECES
    return pl.pallas_call(
        functools.partial(kernel, S, n),
        out_shape=pltpu.VMEM((owned, depth, cells), bf16),
        in_specs=[pl.BlockSpec(memory_space=pl.ANY), pl.BlockSpec(memory_space=pl.ANY)],
        out_specs=pl.BlockSpec(memory_space=pltpu.VMEM),
        scratch_shapes=[
            pltpu.VMEM((chb, depth, cells), bf16),
            pltpu.VMEM((depth, cells, chb), bf16),
            pltpu.VMEM((S, depth, cells, chb), bf16),
            pltpu.VMEM((depth, cells, chb), bf16),
            pltpu.VMEM((planes, 3, cells + 2 * NZ, chb), bf16),
            pltpu.VMEM((owned, TAPS * chb), bf16),
            pltpu.VMEM((planes + 2, cells, owned), f32),
            pltpu.VMEM((PIECES, depth, piece, owned), f32),
            pltpu.VMEM((2, depth, cells // 2, owned), f32),
            pltpu.VMEM((PIECES, depth, piece, owned), f32),
            pltpu.VMEM((PIECES, depth, piece, owned), f32),
            dma(()),
            dma((TAPS,)),
            dma((depth, PIECES)),
            dma((S, depth, PIECES)),
            dma((S, depth, PIECES)),
            dma((S, depth, PIECES)),
            dma((depth, PIECES)),
            dma((depth, PIECES)),
            dma((2, depth, PIECES)),
            dma((PIECES,)),
            dma((PIECES,)),
            dma((2,)),
            dma((2,)),
            dma((PIECES,)),
            dma((PIECES,)),
        ],
        compiler_params=pltpu.CompilerParams(
            collective_id=0, has_side_effects=True, vmem_limit_bytes=62 * 1024 * 1024
        ),
    )(fields, conv_weight)


def general_kernel(
    S, n, r, x_ref, w_ref, out_ref,
    xz, xr, xs, wv, psend, precv, xsend, xrecv, own,
    w_sem, up_sem, down_sem, z_sem, a_send, a_recv, p_send, p_recv, q_send, q_recv,
):
    depth, cells, chb = x_ref.shape
    I = r * chb
    nx = S // 2
    planes = S * depth
    s = lax.axis_index("space")
    z = lax.axis_index("chan")
    x = s // 2
    k = s % 2
    partner = x * 2 + (1 - k)

    for t in range(TAPS):
        pltpu.make_async_copy(w_ref.at[t], wv.at[:, t * I : (t + 1) * I], w_sem.at[t]).start()

    barrier = pltpu.get_barrier_semaphore()

    for so in range(S):
        for step, there in ((-1, z > 0), (1, z < n - 1)):
            @pl.when(there)
            def _():
                pl.semaphore_signal(
                    barrier, inc=1, device_id={"space": lax.rem(s + so, S), "chan": z + step},
                    device_id_type=MESH,
                )

    for so in range(1, S):
        pl.semaphore_signal(
            barrier, inc=1, device_id={"space": lax.rem(s + so, S)}, device_id_type=MESH
        )
    here = jnp.where(z > 0, S, 0) + jnp.where(z < n - 1, S, 0) + (S - 1)
    pl.semaphore_wait(barrier, here)

    split = cells // 2 + NZ
    spans = ((0, split), (split, cells - split))
    rows_out = cells // 2

    def part(ref, u):
        return ref.at[u % depth, pl.ds(*spans[u // depth])]

    def hop(src, b, p, sem, to):
        return pltpu.make_async_remote_copy(
            src_ref=src, dst_ref=part(xz.at[b], p), send_sem=sem, recv_sem=z_sem.at[b, p],
            device_id={"chan": to}, device_id_type=MESH,
        )

    def across(src, b, p):
        return pltpu.make_async_remote_copy(
            src_ref=src, dst_ref=part(xr.at[s, b % r], p), send_sem=a_send.at[b, p],
            recv_sem=a_recv.at[s, b % r, p],
            device_id={"space": b // r}, device_id_type=MESH,
        )

    def source(h, b, p):
        return part(x_ref, p) if h == 0 else part(xz.at[b], p)

    def up(h, p):
        return hop(source(h, z - h, p), z - h, p, up_sem.at[h, p], z + 1)

    def down(h, p):
        return hop(source(h, z + h, p), z + h, p, down_sem.at[h, p], z - 1)

    def slanted(h, b, p, sem, to):
        return pltpu.make_async_remote_copy(
            src_ref=source(h, b, p), dst_ref=part(xr.at[s, b % r], p), send_sem=sem,
            recv_sem=a_recv.at[s, b % r, p],
            device_id={"space": b // r, "chan": to}, device_id_type=MESH,
        )

    def direct(h, b, to, end):
        return (to == end) & (b // r != s)

    def forward(h, p):
        for b, sign, end, send in ((z - h, 1, n - 1, up), (z + h, -1, 0, down)):
            valid = (b >= 0) & (b < n)
            relay = valid
            if h > 0:
                relay = valid & (z != end)

                @pl.when(relay)
                def _():
                    hop(part(xz.at[b], p), b, p, up_sem.at[0, p], z).wait_recv()

            if h < n - 1:
                straight = direct(h, b, z + sign, end)

                @pl.when(valid & (z != end) & ~straight)
                def _():
                    send(h, p).start()

                @pl.when(valid & (z != end) & straight)
                def _():
                    sem = (up_sem if sign == 1 else down_sem).at[h, p]
                    slanted(h, b, p, sem, z + sign).start()

            if h > 0 or sign == 1:
                @pl.when(relay & (b // r != s))
                def _():
                    across(source(h, b, p), b, p).start()

    for p in range(2 * depth):
        forward(0, p)

    zero_row = jnp.zeros((NZ, I), xs.dtype)
    zero_plane = jnp.zeros(xs.shape[2:], xs.dtype)
    for c in range(3):
        xs[0, c] = zero_plane
        xs[planes + 1, c] = zero_plane

        @pl.loop(1, planes + 1)
        def _(q):
            xs[q, c, :NZ, :] = zero_row
            xs[q, c, NZ + cells :, :] = zero_row

    def prepare(ref, u, q, j):
        v = part(ref, u)[...]
        start, size = spans[u // depth]
        rows = lax.broadcasted_iota(jnp.int32, (size, chb), 0) % NZ
        wide = v.astype(jnp.float32)
        before = jnp.where(rows == 0, 0.0, pltpu.roll(wide, 1, 0))
        after = jnp.where(rows == NZ - 1, 0.0, pltpu.roll(wide, size - 1, 0))
        lanes = slice(j * chb, (j + 1) * chb)
        to = slice(NZ + start, NZ + start + size)
        xs[q + 1, 0, to, lanes] = before.astype(xs.dtype)
        xs[q + 1, 1, to, lanes] = v
        xs[q + 1, 2, to, lanes] = after.astype(xs.dtype)

    for half in range(2):
        for h in range(1, n - 1):
            for p in range(depth):
                forward(h, half * depth + p)

    def fetch_half(half):
        for p in range(depth):
            u = half * depth + p
            for j in range(r):
                @pl.when(z == s * r + j)
                def _():
                    prepare(x_ref, u, s * depth + p, j)

                b = s * r + j

                @pl.when(((z == 0) & (b > 0)) | ((z == n - 1) & (b < n - 1)))
                def _():
                    hop(part(xz.at[b], u), b, u, up_sem.at[0, u], z).wait_recv()

                @pl.when(z != s * r + j)
                def _():
                    prepare(xz.at[s * r + j], u, s * depth + p, j)

            @pl.loop(1, S)
            def _(so):
                src = lax.rem(s + so, S)
                for j in range(r):
                    view = part(xr.at[src, j], u)
                    pltpu.make_async_remote_copy(
                        src_ref=view, dst_ref=view,
                        send_sem=a_send.at[0, u], recv_sem=a_recv.at[src, j, u],
                        device_id={"space": src}, device_id_type=MESH,
                    ).wait_recv()
                    prepare(xr.at[src, j], u, src * depth + p, j)

    for t in range(TAPS):
        pltpu.make_async_copy(w_ref.at[t], wv.at[:, t * I : (t + 1) * I], w_sem.at[t]).wait()

    def partial(dest, half):
        window = jnp.concatenate(
            [
                jnp.concatenate(
                    [
                        xs[
                            dest * depth + p + a, c,
                            NZ * b + half * rows_out : NZ * b + (half + 1) * rows_out, :,
                        ]
                        for p in range(depth)
                    ],
                    axis=0,
                )
                for a in range(3)
                for b in range(3)
                for c in range(3)
            ],
            axis=1,
        )
        return lax.dot_general(
            window, wv[...], (((1,), (1,)), ((), ())), preferred_element_type=jnp.float32
        )

    def target(hops, mine):
        far = lax.rem(x + hops, nx)
        return far * 2 + jnp.where(mine == 1, k, 1 - k)

    def half_of(ref, m, half):
        return ref.at[m, half]

    def to_partner(m, half):
        return pltpu.make_async_remote_copy(
            src_ref=half_of(psend, m, half), dst_ref=half_of(precv, m, half),
            send_sem=p_send.at[m, half], recv_sem=p_recv.at[m, half],
            device_id={"space": partner}, device_id_type=MESH,
        )

    def to_chip(m, half, there):
        return pltpu.make_async_remote_copy(
            src_ref=half_of(xsend, m, half), dst_ref=half_of(xrecv, m, half),
            send_sem=q_send.at[m, half], recv_sem=q_recv.at[m, half],
            device_id={"space": there}, device_id_type=MESH,
        )

    def reduce_half(half, first, stop):
        @pl.loop(2 * first, 2 * stop)
        def _(i):
            m = i // 2
            mine = i % 2
            total = partial(target(m + 1, mine), half)

            @pl.when(mine == 0)
            def _():
                psend[m, half] = total
                to_partner(m, half).start()

            @pl.when(mine == 1)
            def _():
                to_partner(m, half).wait_recv()
                if first < nx - 1:
                    xsend[m, half] = total + precv[m, half]
                    to_chip(m, half, target(m + 1, 1)).start()
                else:
                    own[half] = total + precv[m, half]

    fetch_half(0)
    reduce_half(0, 0, nx - 1)
    fetch_half(1)
    reduce_half(1, 0, nx - 1)
    for half in range(2):
        reduce_half(half, nx - 1, nx)

    for half in range(2):
        total = own[half]
        for m in range(nx - 1):
            to_chip(m, half, partner).wait_recv()
            total = total + xrecv[m, half]
        for p in range(depth):
            out_ref[p, half * rows_out : (half + 1) * rows_out, :] = total[
                p * rows_out : (p + 1) * rows_out
            ].astype(out_ref.dtype)

    for h in range(n):
        for p in range(2 * depth):
            if h < n - 1:
                @pl.when((z - h >= 0) & (z < n - 1))
                def _():
                    up(h, p).wait_send()

                @pl.when((z + h < n) & (z > 0))
                def _():
                    down(h, p).wait_send()

            for b, sign, end in ((z - h, 1, n - 1), (z + h, -1, 0)):
                relay = (b >= 0) & (b < n) & (b // r != s)
                if h > 0:
                    relay = relay & ~direct(h - 1, b, z, end)

                if h > 0 or sign == 1:
                    @pl.when(relay)
                    def _():
                        across(source(h, b, p), b, p).wait_send()

    for m in range(nx):
        for half in range(2):
            to_partner(m, half).wait_send()
            if m < nx - 1:
                to_chip(m, half, partner).wait_send()


def general(S, n, fields, conv_weight):
    chb, depth, cells = fields.shape
    owned, I = conv_weight.shape[1:]
    r = I // chb
    nx = S // 2
    planes = S * depth
    bf16, f32 = jnp.bfloat16, jnp.float32
    dma = pltpu.SemaphoreType.DMA
    x = jnp.transpose(fields, (1, 2, 0))
    result = pl.pallas_call(
        functools.partial(general_kernel, S, n, r),
        out_shape=jax.ShapeDtypeStruct((depth, cells, owned), bf16),
        in_specs=[
            pl.BlockSpec(memory_space=pltpu.VMEM),
            pl.BlockSpec(memory_space=pl.ANY),
        ],
        out_specs=pl.BlockSpec(memory_space=pltpu.VMEM),
        scratch_shapes=[
            pltpu.VMEM((n, depth, cells, chb), bf16),
            pltpu.VMEM((S, r, depth, cells, chb), bf16),
            pltpu.VMEM((planes + 2, 3, cells + 2 * NZ, I), bf16),
            pltpu.VMEM((owned, TAPS * I), bf16),
            pltpu.VMEM((nx, 2, depth * cells // 2, owned), f32),
            pltpu.VMEM((nx, 2, depth * cells // 2, owned), f32),
            pltpu.VMEM((nx - 1, 2, depth * cells // 2, owned), f32),
            pltpu.VMEM((nx - 1, 2, depth * cells // 2, owned), f32),
            pltpu.VMEM((2, depth * cells // 2, owned), f32),
            dma((TAPS,)),
            dma((n, 2 * depth)),
            dma((n, 2 * depth)),
            dma((n, 2 * depth)),
            dma((n, 2 * depth)),
            dma((S, r, 2 * depth)),
            dma((nx, 2)),
            dma((nx, 2)),
            dma((nx, 2)),
            dma((nx, 2)),
        ],
        compiler_params=pltpu.CompilerParams(
            collective_id=0, has_side_effects=True, vmem_limit_bytes=62 * 1024 * 1024
        ),
    )(x, conv_weight)
    return jnp.transpose(result, (2, 0, 1))


def solution(mesh):
    return jax.shard_map(
        functools.partial(local, mesh.shape["space"], mesh.shape["chan"]),
        mesh=mesh,
        in_specs=(P("chan", ("groups", "space"), None), P(None, "chan", "space")),
        out_specs=P("chan", ("groups", "space"), None),
        check_vma=False,
    )
```
